256 devices in a mesh: ctx: 64 (over y_lo, x, z), head: 4 (over y_hi, core).
Axes of the slice: x: 4, y: 4 (y_hi: 2, y_lo: 2; y = y_hi * 2 + y_lo), z: 8, core: 2. Of those that a mesh axis runs over, the one named last changes fastest.
Arguments:
- queries: bfloat16 [12288, 768], P(('ctx', 'head')), may hold values from -2.5 to 2.5
- keys: bfloat16 [12288, 768], P(('ctx', 'head')), may hold values from -2.5 to 2.5
- values: bfloat16 [12288, 768], P(('ctx', 'head')), may hold values from -6 to 6
- attended: bfloat16 [12288, 768], P(('ctx', 'head')), may hold values from -6 to 6
- grad_out: bfloat16 [12288, 768], P(('ctx', 'head')), may hold values from -6 to 6
- logsumexp: float32 [12288, 12], P('ctx', 'head'), may hold values from 5 to 8
Outputs:
- grad_queries: bfloat16 [12288, 768], P(('ctx', 'head'))
- grad_keys: bfloat16 [12288, 768], P(('ctx', 'head'))
- grad_values: bfloat16 [12288, 768], P(('ctx', 'head'))
The draws below stay inside these ranges and needn't reach their ends.
All inputs are finite; a program needn't handle non-finite values.
Results may differ from the reference program's by a relative error of at most 0.0051.
Values may be sent and summed in bfloat16 or wider, within the bound.
A program may use at most 128 MiB of HBM per device.

```python
import math
import jax
import jax.numpy as jnp
from jax import lax

HEADS = 12
HEAD_DIM = 64
WIDTH = 768
SEQ = 12288


def levels(own_key, extent, pieces, smallest, largest):
    level = 1.0
    for axis_at, parts in pieces:
        heights = jax.random.uniform(jax.random.fold_in(jax.random.fold_in(own_key, 6), axis_at), (parts,), jnp.float32, smallest / len(pieces), largest / len(pieces))
        level = level * jnp.repeat(jnp.exp(heights), extent[axis_at] // parts).reshape((-1,) + (1,) * (len(extent) - 1 - axis_at))
    return level


def scatter_about(key, dims, spread, bound, cuts=(), kind=jnp.bfloat16):
    values = jax.random.normal(key, dims, jnp.float32) * spread
    if len(cuts) > 0:
        values = levels(key, dims, cuts, -0.22, 0.18) * values
    return jnp.clip(values, min=-bound, max=bound).astype(kind)


def setup_inputs(seed: int = 0) -> dict:
    splits = jax.random.split(jax.random.key(seed), 7)
    queries = scatter_about(splits[0], (SEQ, WIDTH), 1.0, 2.5, ((0, 256),))
    keys = scatter_about(splits[1], (SEQ, WIDTH), 1.0, 2.5, ((0, 256),))
    values = scatter_about(splits[2], (SEQ, WIDTH), 1.0, 6.0, ((0, 256),))
    attended = scatter_about(splits[3], (SEQ, WIDTH), 1.0, 6.0, ((0, 256),))
    grad_out = scatter_about(splits[4], (SEQ, WIDTH), 1.0, 6.0, ((0, 256),))
    logsumexp = jnp.clip(5.0 + 3.0 * jax.random.uniform(splits[5], (SEQ, HEADS), jnp.float32) ** levels(splits[5], (SEQ, HEADS), ((0, 64), (1, 4)), -0.2, 0.2), 5.0, 8.0)
    return {"queries": queries, "keys": keys, "values": values, "attended": attended, "grad_out": grad_out, "logsumexp": logsumexp}


def reference(queries, keys, values, attended, grad_out, logsumexp):
    scaling = HEAD_DIM ** -0.5
    length = queries.shape[0]

    def by_head(matrix):
        return matrix.astype(jnp.float32).reshape(length, HEADS, HEAD_DIM)

    local_q = by_head(queries)
    local_k = by_head(keys)
    local_v = by_head(values)
    local_o = by_head(attended)
    local_g = by_head(grad_out)
    deltas = jnp.sum(local_g * local_o, axis=2)
    block_size = math.gcd(length, 256)
    block_count = length // block_size

    def visit(totals, inputs):
        grad_key, grad_value = totals
        query_part, grad_part, norm_part, delta_part = inputs
        scores = jnp.einsum("ahd,bhd->hab", query_part, local_k) * scaling
        weights = jnp.exp(scores - jnp.transpose(norm_part)[:, :, None])
        weights_low = lax.optimization_barrier(weights.astype(jnp.bfloat16)).astype(jnp.float32)
        dweights = jnp.einsum("ahd,bhd->hab", grad_part, local_v)
        dscores = weights * (dweights - jnp.transpose(delta_part)[:, :, None])
        dscores = lax.optimization_barrier(dscores.astype(jnp.bfloat16)).astype(jnp.float32)
        grad_query = jnp.einsum("hab,bhd->ahd", dscores, local_k) * scaling
        grad_key = grad_key + jnp.einsum("hab,ahd->bhd", dscores, query_part) * scaling
        grad_value = grad_value + jnp.einsum("hab,ahd->bhd", weights_low, grad_part)
        return (grad_key, grad_value), grad_query

    zeros = jnp.zeros((length, HEADS, HEAD_DIM), jnp.float32)
    stacked = (
        local_q.reshape(block_count, block_size, HEADS, HEAD_DIM),
        local_g.reshape(block_count, block_size, HEADS, HEAD_DIM),
        logsumexp.reshape(block_count, block_size, HEADS),
        deltas.reshape(block_count, block_size, HEADS),
    )
    totals, grad_query = lax.scan(visit, (zeros, zeros), stacked)

    def finish(matrix):
        return matrix.reshape(length, HEADS * HEAD_DIM).astype(jnp.bfloat16)

    return finish(grad_query), finish(totals[0]), finish(totals[1])
```

```python
import functools

import jax
import jax.numpy as jnp
from jax import lax
from jax.experimental import pallas as pl
from jax.experimental.pallas import tpu as pltpu
from jax.sharding import PartitionSpec as P

F32 = jnp.float32
BF16 = jnp.bfloat16
MESH = pl.DeviceIdType.MESH

NX, NY, NZ = 4, 4, 8
HL = 3
D = 64
SUB = 48
CH = NY * SUB
NI = NZ * CH
NJ = 2 * NX * CH
HALF = NJ // 2
Z_SLOT = {0: 0, 1: 1, -1: 2, 2: 3, -2: 4, 3: 5, -3: 6, 4: 7}
X_SLOT = {0: 0, 1: 1, -1: 2, 2: 3}
PK = CH + CH // 2
BJ = 512


def nt(a, b):
    return lax.dot_general(a, b, (((1,), (1,)), ((), ())), preferred_element_type=F32)


def tn(a, b):
    return lax.dot_general(a, b, (((0,), (0,)), ((), ())), preferred_element_type=F32)


def nn(a, b):
    return jnp.dot(a, b, preferred_element_type=F32)


def kernel(
    q_ref, k_ref, v_ref, o_ref, g_ref, lse_ref, dq_ref, dk_ref, dv_ref,
    st_qg, st_kv, st_d, qg, kv, r_lse, r_d, stat, stat_all, dqt, dkv, dkv16, r_core, x16, r_x,
    dq16, r_q, fin, r_fin,
    a_send, a_recv, l_send, l_recv, z_send, z_recv, x_send, x_recv, c_send, c_recv,
    kc_send, kc_recv, kx_send, kx_recv, q_send, q_recv, f_send, f_recv,
):
    c = lax.axis_index("ctx")
    g = lax.axis_index("head")
    z = c % NZ
    x = (c // NZ) % NX
    y_lo = c // (NZ * NX)
    y_hi = g // 2
    core = g % 2
    y = 2 * y_hi + y_lo

    def dev(dx=0, dy=0, dz=0, other=False):
        yy = (y + dy) % NY
        cc = (yy % 2) * (NX * NZ) + ((x + dx + NX) % NX) * NZ + (z + dz + NZ) % NZ
        return (cc, (yy // 2) * 2 + (1 - core if other else core))

    def remote(src, dst, send, recv, to):
        return pltpu.make_async_remote_copy(
            src_ref=src, dst_ref=dst, send_sem=send, recv_sem=recv, device_id=to,
            device_id_type=MESH,
        )

    barrier = pltpu.get_barrier_semaphore()
    peers = [dev(dy=dy, other=o) for dy in range(NY) for o in (False, True) if dy or o]
    peers += [dev(dz=d) for d in Z_SLOT if d] + [dev(dx=d) for d in X_SLOT if d]
    for peer in peers:
        pl.semaphore_signal(barrier, inc=1, device_id=peer, device_id_type=MESH)

    qs = q_ref[...] * jnp.asarray(0.125, BF16)
    ks, vs, gs = k_ref[...], v_ref[...], g_ref[...]
    for n in range(NY * HL):
        cols = slice(n * D, (n + 1) * D)
        st_qg[n // HL, n % HL] = jnp.concatenate([qs[:, cols], gs[:, cols]], axis=1)
        st_kv[n // HL, n % HL] = jnp.concatenate([ks[:, cols], vs[:, cols]], axis=1)
    prod = gs.astype(F32) * o_ref[...].astype(F32)
    hi = prod.astype(BF16)
    lo = (prod - hi.astype(F32)).astype(BF16)
    row = lax.broadcasted_iota(jnp.int32, (8 * NY, NY * HL * D), 0)
    col = lax.broadcasted_iota(jnp.int32, (8 * NY, NY * HL * D), 1)
    start = ((row // 8) * HL + row % 8) * D
    pick = ((row % 8 < HL) & (col >= start) & (col < start + D)).astype(F32).astype(BF16)
    deltas = nt(pick, hi) + nt(pick, lo)
    for n in range(NY):
        st_d[n] = deltas[8 * n : 8 * n + 8]

    pl.semaphore_wait(barrier, len(peers))

    first = []
    for r in range(1, NY):
        to = dev(dy=r)
        group = (y + r) % NY
        rows = pl.ds((NY - r) * SUB, SUB)
        first += [
            remote(st_qg.at[group], qg.at[:, rows], a_send.at[r, 0], a_recv.at[r, 0], to),
            remote(st_kv.at[group], kv.at[:, rows], a_send.at[r, 1], a_recv.at[r, 1], to),
            remote(st_d.at[group], r_d.at[NY - r], a_send.at[r, 2], a_recv.at[r, 2], to),
        ]
    for copy in first:
        copy.start()
    lse_to = (g % 2) * (NX * NZ) + x * NZ + z
    lse_own = core == y_lo

    def lse_copy(score):
        return remote(
            lse_ref.at[score], r_lse.at[y_lo], l_send.at[score], l_recv.at[y_lo],
            (lse_to, (g // 2) * 2 + score),
        )

    def lse_local(score):
        return lse_own & (core == score)

    for score in range(2):

        @pl.when(jnp.logical_not(lse_local(score)))
        def _():
            lse_copy(score).start()

        @pl.when(lse_local(score))
        def _():
            r_lse[y_lo] = lse_ref[score]

    qg[:, 0:SUB] = st_qg[y]
    kv[:, 0:SUB] = st_kv[y]
    r_d[0] = st_d[y]
    for copy in first:
        copy.wait_recv()
    for source in range(2):

        @pl.when(jnp.logical_not(lse_own & (source == y_lo)))
        def _():
            remote(
                lse_ref.at[0], r_lse.at[source], l_send.at[0], l_recv.at[source],
                (lse_to, (g // 2) * 2),
            ).wait_recv()

    for r in range(NY):
        from_y = (y + r) % NY
        stat[0, 0:8, r * SUB : (r + 1) * SUB] = r_lse[from_y % 2, from_y // 2]
        stat[0, 8:16, r * SUB : (r + 1) * SUB] = r_d[r]

    def z_copies(step, sign):
        d = -sign * (step - 1)
        arrives = d - sign
        if step == NZ // 2:
            arrives, part = 4, CH // 2
            offset = 0 if sign > 0 else part
        else:
            part, offset = CH, 0
        a, b = Z_SLOT[d], Z_SLOT[arrives]
        way = 0 if sign > 0 else 1
        copies = [
            remote(
                qg.at[:, pl.ds(a * CH + offset, part)], qg.at[:, pl.ds(b * CH + offset, part)],
                z_send.at[way, step, 0], z_recv.at[way, step, 0], dev(dz=sign),
            )
        ]
        if step < NZ // 2 or sign > 0:
            copies.append(
                remote(
                    stat.at[a], stat.at[b], z_send.at[way, step, 1], z_recv.at[way, step, 1],
                    dev(dz=sign),
                )
            )
        return copies

    def x_copies(step, sign):
        d = -sign * (step - 1)
        arrives = d - sign
        if step == NX // 2:
            arrives, part = 2, CH // 2
            offset = 0 if sign > 0 else part
        else:
            part, offset = CH, 0
        a, b = X_SLOT[d], X_SLOT[arrives]
        way = 0 if sign > 0 else 1
        return [
            remote(
                kv.at[:, pl.ds(a * CH + offset, part)], kv.at[:, pl.ds(b * CH + offset, part)],
                x_send.at[way, step], x_recv.at[way, step], dev(dx=sign),
            )
        ]

    def core_copy(slot):
        return remote(
            kv.at[:, pl.ds(slot * CH, CH)], kv.at[:, pl.ds(HALF + slot * CH, CH)],
            c_send.at[slot], c_recv.at[slot], dev(other=True),
        )

    sent = []
    zs = {}
    for step in range(1, NZ // 2 + 1):
        for sign in (1, -1):
            if step > 1:
                for copy in zs[step - 1, sign]:
                    copy.wait_recv()
            zs[step, sign] = z_copies(step, sign)
            for copy in zs[step, sign]:
                copy.start()
            sent += zs[step, sign]
        if step == 1:
            xs = x_copies(1, 1) + x_copies(1, -1) + [core_copy(0)]
            for copy in xs:
                copy.start()
        if step == 2:
            xs[0].wait_recv()
            xs[1].wait_recv()
            more = x_copies(2, 1) + x_copies(2, -1) + [core_copy(1), core_copy(2)]
            for copy in more:
                copy.start()
        if step == 3:
            more[0].wait_recv()
            more[1].wait_recv()
            last = core_copy(3)
            last.start()
    for sign in (1, -1):
        for copy in zs[NZ // 2, sign]:
            copy.wait_recv()
    for copy in [xs[2], more[2], more[3], last]:
        copy.wait_recv()
    sent += xs + more + [last]
    for slot in range(NZ):
        stat_all[:, slot * CH : (slot + 1) * CH] = stat[slot]

    lane = lax.broadcasted_iota(jnp.int32, (BJ, 2 * D), 1)

    @pl.loop(0, HL)
    def _(h):
        norms = stat_all[pl.ds(h, 1), :]
        dels = stat_all[pl.ds(8 + h, 1), :]
        rows_q = qg[h]
        for jb in range(NJ // BJ):
            js = slice(jb * BJ, (jb + 1) * BJ)
            both = kv[h, js]
            zero = jnp.zeros_like(both)
            scores = nt(jnp.where(lane < D, both, zero), rows_q)
            dweights = nt(jnp.where(lane < D, zero, both), rows_q)
            weights = jnp.exp(scores - norms)
            dscores = (weights * (dweights - dels)).astype(BF16)
            low = weights.astype(BF16)
            dkv[h, js] = jnp.where(lane < D, nn(dscores, rows_q), nn(low, rows_q))
            term = tn(both, dscores)[:D]
            if jb == 0:
                dqt[h] = term
            else:
                dqt[h] += term

    dkv16[...] = dkv[:, HALF:].astype(BF16)
    kc = remote(dkv16, r_core, kc_send, kc_recv, dev(other=True))
    kc.start()
    for s in range(NI // 384):
        block = jnp.transpose(dqt[:, :, s * 384 : (s + 1) * 384].reshape(HL * D, 384))
        block = (block * 0.125).astype(BF16)
        for t in range(2):
            piece = block[t * CH : (t + 1) * CH]
            dq16[2 * s + t, 0:CH] = piece[:, : 2 * D]
            dq16[2 * s + t, CH:PK] = jnp.concatenate(
                [piece[: CH // 2, 2 * D :], piece[CH // 2 :, 2 * D :]], axis=1
            )
    qc = []
    for d, slot in Z_SLOT.items():
        if d:
            back = Z_SLOT[4 if d == 4 else -d]
            qc.append(
                remote(dq16.at[slot], r_q.at[back], q_send.at[slot], q_recv.at[slot], dev(dz=d))
            )
    for copy in qc:
        copy.start()
    kc.wait_recv()
    dkv[:, :HALF] = dkv[:, :HALF] + r_core[...].astype(F32)
    x16[...] = dkv[:, CH:HALF].astype(BF16)
    xc = []
    for d, slot in X_SLOT.items():
        if d:
            back = X_SLOT[2 if d == 2 else -d]
            xc.append(
                remote(
                    x16.at[:, pl.ds((slot - 1) * CH, CH)], r_x.at[back - 1], kx_send.at[slot],
                    kx_recv.at[slot], dev(dx=d),
                )
            )
    for copy in xc:
        copy.start()
    for copy in qc:
        copy.wait_recv()
    total_q = dq16[0].astype(F32)
    for slot in range(1, NZ):
        total_q = total_q + r_q[slot].astype(F32)
    for copy in xc:
        copy.wait_recv()
    for r in range(NY):
        rows = slice(r * SUB, (r + 1) * SUB)
        for h in range(HL):
            total = dkv[h, rows]
            for slot in range(NX - 1):
                total = total + r_x[slot, h, rows].astype(F32)
            fin[r, :, h * 2 * D : (h + 1) * 2 * D] = total.astype(BF16)
        fin[r, :, 6 * D : 8 * D] = total_q[rows].astype(BF16)
        at = CH + (r % 2) * SUB
        side = total_q[at : at + SUB]
        fin[r, :, 8 * D : 9 * D] = side[:, (r // 2) * D : (r // 2 + 1) * D].astype(BF16)

    fc = [
        remote(fin.at[r], r_fin.at[y], f_send.at[r], f_recv.at[r], dev(dy=r)) for r in range(1, NY)
    ]
    for copy in fc:
        copy.start()
    r_fin[y] = fin[0]
    for copy in fc:
        copy.wait_recv()
    for n in range(NY):
        for h in range(HL):
            cols = slice((n * HL + h) * D, (n * HL + h + 1) * D)
            pair = r_fin[n, :, h * 2 * D : (h + 1) * 2 * D]
            dk_ref[:, cols] = pair[:, :D]
            dv_ref[:, cols] = pair[:, D:]
            dq_ref[:, cols] = r_fin[n, :, (6 + h) * D : (7 + h) * D]
    for copy in first + sent + [kc] + qc + xc + fc:
        copy.wait_send()
    for score in range(2):

        @pl.when(jnp.logical_not(lse_local(score)))
        def _():
            lse_copy(score).wait_send()


def local(queries, keys, values, attended, grad_out, logsumexp):
    norms = jnp.pad(jnp.transpose(logsumexp), ((0, 8 - HL), (0, 0)))
    norms = norms.reshape(8, 2, 2, SUB).transpose(2, 1, 0, 3)
    out = jax.ShapeDtypeStruct(queries.shape, BF16)
    dma = pltpu.SemaphoreType.DMA
    vm = pltpu.VMEM
    return pl.pallas_call(
        kernel,
        out_shape=(out, out, out),
        in_specs=[pl.BlockSpec(memory_space=pltpu.VMEM)] * 6,
        out_specs=[pl.BlockSpec(memory_space=pltpu.VMEM)] * 3,
        scratch_shapes=[
            vm((NY, HL, SUB, 2 * D), BF16),
            vm((NY, HL, SUB, 2 * D), BF16),
            vm((NY, 8, SUB), F32),
            vm((HL, NI, 2 * D), BF16),
            vm((HL, NJ, 2 * D), BF16),
            vm((2, 2, 8, SUB), F32),
            vm((NY, 8, SUB), F32),
            vm((NZ, 16, CH), F32),
            vm((16, NI), F32),
            vm((HL, D, NI), F32),
            vm((HL, NJ, 2 * D), F32),
            vm((HL, HALF, 2 * D), BF16),
            vm((HL, HALF, 2 * D), BF16),
            vm((HL, HALF - CH, 2 * D), BF16),
            vm((NX - 1, HL, CH, 2 * D), BF16),
            vm((NZ, PK, 2 * D), BF16),
            vm((NZ, PK, 2 * D), BF16),
            vm((NY, SUB, 10 * D), BF16),
            vm((NY, SUB, 10 * D), BF16),
            dma((NY, 3)), dma((NY, 3)),
            dma((2,)), dma((2,)),
            dma((2, NZ // 2 + 1, 2)), dma((2, NZ // 2 + 1, 2)),
            dma((2, NX // 2 + 1)), dma((2, NX // 2 + 1)),
            dma((NX,)), dma((NX,)),
            dma, dma,
            dma((NX,)), dma((NX,)),
            dma((NZ,)), dma((NZ,)),
            dma((NY,)), dma((NY,)),
        ],
        compiler_params=pltpu.CompilerParams(
            collective_id=0, has_side_effects=True, vmem_limit_bytes=56 << 20
        ),
        name="attention_grad",
    )(queries, keys, values, attended, grad_out, norms)


def solution(mesh):
    rows = P(("ctx", "head"), None)
    return jax.shard_map(
        local,
        mesh=mesh,
        in_specs=(rows,) * 5 + (P("ctx", "head"),),
        out_specs=(rows,) * 3,
        check_vma=False,
    )
```

```python
import functools

import jax
import jax.numpy as jnp
from jax import lax
from jax.experimental import pallas as pl
from jax.experimental.pallas import tpu as pltpu
from jax.sharding import PartitionSpec as P

F32 = jnp.float32
BF16 = jnp.bfloat16
MESH = pl.DeviceIdType.MESH

NX, NY, NZ = 4, 4, 8
HL = 3
D = 64
SUB = 48
CH = NY * SUB
NI = NZ * CH
NJ = 2 * NX * CH
HALF = NJ // 2
Z_SLOT = {0: 0, 1: 1, -1: 2, 2: 3, -2: 4, 3: 5, -3: 6, 4: 7}
X_SLOT = {0: 0, 1: 1, -1: 2, 2: 3}
PK = CH // 2


def nt(a, b):
    return lax.dot_general(a, b, (((1,), (1,)), ((), ())), preferred_element_type=F32)


def tn(a, b):
    return lax.dot_general(a, b, (((0,), (0,)), ((), ())), preferred_element_type=F32)


def nn(a, b):
    return jnp.dot(a, b, preferred_element_type=F32)


def kernel(
    q_ref, k_ref, v_ref, o_ref, g_ref, lse_ref, out_kv, out_q,
    st_qg, st_kv, st_d, st_lse, qg, kv, r_lse, r_d, stat, stat_all, dqt, dkv, dkv16, r_core, x16,
    r_x, dq16, r_q, fin_kv, fin_q, r_kv, r_fq,
    a_send, a_recv, l_send, l_recv, z_send, z_recv, s_send, s_recv, x_send, x_recv, c_send, c_recv,
    kc_send, kc_recv, kx_send, kx_recv, q_send, q_recv, f_send, f_recv,
):
    c = lax.axis_index("ctx")
    g = lax.axis_index("head")
    z = c % NZ
    x = (c // NZ) % NX
    y_lo = c // (NZ * NX)
    y_hi = g // 2
    core = g % 2
    y = 2 * y_hi + y_lo

    def dev(dx=0, dy=0, dz=0, other=False):
        yy = (y + dy) % NY
        cc = (yy % 2) * (NX * NZ) + ((x + dx + NX) % NX) * NZ + (z + dz + NZ) % NZ
        return (cc, (yy // 2) * 2 + (1 - core if other else core))

    def remote(src, dst, send, recv, to):
        return pltpu.make_async_remote_copy(
            src_ref=src, dst_ref=dst, send_sem=send, recv_sem=recv, device_id=to,
            device_id_type=MESH,
        )

    def start(copies):
        for copy in copies:
            copy.start()

    def arrive(copies):
        for copy in copies:
            copy.wait_recv()

    barrier = pltpu.get_barrier_semaphore()
    peers = [dev(dy=dy, other=o) for dy in range(NY) for o in (False, True) if dy or o]
    peers += [dev(dz=d) for d in Z_SLOT if d] + [dev(dx=d) for d in X_SLOT if d]
    for peer in peers:
        pl.semaphore_signal(barrier, inc=1, device_id=peer, device_id_type=MESH)

    def y_copy(r, kind):
        group = (y + r) % NY
        rows = pl.ds((NY - r) * SUB, SUB)
        src = (st_qg, st_kv, st_d)[kind].at[group]
        dst = (qg.at[:, rows], kv.at[:, rows], r_d.at[NY - r])[kind]
        return remote(src, dst, a_send.at[r, kind], a_recv.at[r, kind], dev(dy=r))

    def ring(buf, slots, axis, last, step, sign, r, send, recv):
        d = -sign * (step - 1)
        a = slots[d]
        b = slots[last if step == last else d - sign]
        way = 0 if sign > 0 else 1
        return remote(
            buf.at[:, pl.ds(a * CH + r * SUB, SUB)], buf.at[:, pl.ds(b * CH + r * SUB, SUB)],
            send.at[way, step, r], recv.at[way, step, r], dev(**{axis: sign}),
        )

    def z_copy(step, sign, r):
        return ring(qg, Z_SLOT, "dz", NZ // 2, step, sign, r, z_send, z_recv)

    def x_copy(step, sign, r):
        return ring(kv, X_SLOT, "dx", NX // 2, step, sign, r, x_send, x_recv)

    def halves(step, last, sign):
        return range(NY) if step < last else ((0, 1) if sign > 0 else (2, 3))

    def s_copy(step, sign):
        d = -sign * (step - 1)
        way = 0 if sign > 0 else 1
        return remote(
            stat.at[Z_SLOT[d]], stat.at[Z_SLOT[4 if step == NZ // 2 else d - sign]],
            s_send.at[way, step], s_recv.at[way, step], dev(dz=sign),
        )

    def c_copy(i):
        begin, rows = [(r * SUB, SUB) for r in range(NY)][i] if i < NY else (
            ((i - 3) * CH, CH) if i < 6 else (3 * CH + (i - 6) * (CH // 2), CH // 2)
        )
        return remote(
            kv.at[:, pl.ds(begin, rows)], kv.at[:, pl.ds(HALF + begin, rows)],
            c_send.at[i], c_recv.at[i], dev(other=True),
        )

    lse_to = (g % 2) * (NX * NZ) + x * NZ + z
    lse_own = core == y_lo

    def lse_copy(score):
        return remote(
            st_lse.at[score], r_lse.at[y_lo], l_send.at[score], l_recv.at[y_lo],
            (lse_to, (g // 2) * 2 + score),
        )

    def lse_local(score):
        return lse_own & (core == score)

    def stage(st, left, right):
        for n in range(NY * HL):
            cols = slice(n * D, (n + 1) * D)
            st[n // HL, n % HL] = jnp.concatenate([left[:, cols], right[:, cols]], axis=1)

    order = (1, 3, 2)
    stage(st_kv, k_ref[...], v_ref[...])
    pl.semaphore_wait(barrier, len(peers))
    start([y_copy(r, 1) for r in order])
    kv[:, 0:SUB] = st_kv[y]
    start([x_copy(1, 1, 0), x_copy(1, -1, 0), c_copy(0)])
    gs = g_ref[...]
    stage(st_qg, q_ref[...] * jnp.asarray(0.125, BF16), gs)
    start([y_copy(r, 0) for r in order])
    qg[:, 0:SUB] = st_qg[y]
    start([z_copy(1, 1, 0), z_copy(1, -1, 0)])
    prod = gs.astype(F32) * o_ref[...].astype(F32)
    hi = prod.astype(BF16)
    lo = (prod - hi.astype(F32)).astype(BF16)
    row = lax.broadcasted_iota(jnp.int32, (8 * NY, NY * HL * D), 0)
    col = lax.broadcasted_iota(jnp.int32, (8 * NY, NY * HL * D), 1)
    begin = ((row // 8) * HL + row % 8) * D
    pick = ((row % 8 < HL) & (col >= begin) & (col < begin + D)).astype(F32).astype(BF16)
    deltas = nt(pick, hi) + nt(pick, lo)
    for n in range(NY):
        st_d[n] = deltas[8 * n : 8 * n + 8]
    start([y_copy(r, 2) for r in order])
    st_lse[...] = jnp.zeros_like(st_lse)
    for s in range(NY):
        st_lse[s % 2, s // 2, 0:HL] = lse_ref[:, s * SUB : (s + 1) * SUB]
    for score in range(2):

        @pl.when(jnp.logical_not(lse_local(score)))
        def _():
            lse_copy(score).start()

        @pl.when(lse_local(score))
        def _():
            r_lse[y_lo] = st_lse[score]

    r_d[0] = st_d[y]
    dqt[...] = jnp.zeros_like(dqt)
    dkv[...] = jnp.zeros_like(dkv)

    for r, kind in ((1, 1), (3, 1), (1, 0), (3, 0), (2, 1), (2, 0)):
        y_copy(NY - r, kind).wait_recv()
        if kind == 1:
            start([x_copy(1, 1, r), x_copy(1, -1, r), c_copy(r)])
        else:
            start([z_copy(1, 1, r), z_copy(1, -1, r)])
    for r in range(1, NY):
        y_copy(r, 2).wait_recv()
    for source in range(2):

        @pl.when(jnp.logical_not(lse_own & (source == y_lo)))
        def _():
            remote(
                st_lse.at[0], r_lse.at[source], l_send.at[0], l_recv.at[source],
                (lse_to, (g // 2) * 2),
            ).wait_recv()

    for r in range(NY):
        from_at = (y + r) % NY
        stat[0, 0:8, r * SUB : (r + 1) * SUB] = r_lse[from_at % 2, from_at // 2]
        stat[0, 8:16, r * SUB : (r + 1) * SUB] = r_d[r]
    start([s_copy(1, 1), s_copy(1, -1)])
    for r in (0, 1, 3, 2):
        for sign in (1, -1):
            x_copy(1, sign, r).wait_recv()
            if r in halves(2, 2, sign):
                x_copy(2, sign, r).start()
        for sign in (1, -1):
            z_copy(1, sign, r).wait_recv()
            z_copy(2, sign, r).start()
    start([c_copy(4), c_copy(5)])
    for sign in (1, -1):
        s_copy(1, sign).wait_recv()
        s_copy(2, sign).start()
    for sign, i in ((1, 6), (-1, 7)):
        arrive([x_copy(2, sign, r) for r in halves(2, 2, sign)])
        c_copy(i).start()
    for r in (0, 1, 3, 2):
        for sign in (1, -1):
            z_copy(2, sign, r).wait_recv()
            z_copy(3, sign, r).start()
    for sign in (1, -1):
        s_copy(2, sign).wait_recv()
        s_copy(3, sign).start()

    def join(slots):
        for slot in slots:
            stat_all[:, slot * CH : (slot + 1) * CH] = stat[slot]

    join(range(4))

    def q_copy(h, d):
        slot = Z_SLOT[d]
        back = Z_SLOT[4 if d == 4 else -d]
        return remote(
            dq16.at[h, slot], r_q.at[h, back], q_send.at[h, slot], q_recv.at[h, slot], dev(dz=d)
        )

    def send_dq(h, half):
        cols = slice(half * 4 * CH, (half + 1) * 4 * CH)
        block = (jnp.transpose(dqt[h, :, cols]) * 0.125).astype(BF16)
        for t in range(4):
            piece = block[t * CH : (t + 1) * CH]
            dq16[h, 4 * half + t] = jnp.concatenate([piece[:PK], piece[PK:]], axis=1)
        start([q_copy(h, d) for d, slot in Z_SLOT.items() if d and slot // 4 == half])

    def kc_copy(h):
        return remote(dkv16.at[h], r_core.at[h], kc_send.at[h], kc_recv.at[h], dev(other=True))

    def send_core(h):
        dkv16[h] = dkv[h, HALF:].astype(BF16)
        kc_copy(h).start()

    def kx_copy(h, d):
        slot = X_SLOT[d]
        back = X_SLOT[2 if d == 2 else -d]
        return remote(
            x16.at[h, pl.ds((slot - 1) * CH, CH)], r_x.at[h, back - 1], kx_send.at[h, slot],
            kx_recv.at[h, slot], dev(dx=d),
        )

    def send_x(h):
        kc_copy(h).wait_recv()
        total = dkv[h, :HALF] + r_core[h].astype(F32)
        x16[h] = total[CH:].astype(BF16)
        start([kx_copy(h, d) for d in X_SLOT if d])
        dkv[h, :CH] = total[:CH]

    lane = lax.broadcasted_iota(jnp.int32, (HALF, 2 * D), 1)

    @pl.loop(0, 4 * HL)
    def _(t):
        h = (t + 2) % HL
        late = jnp.where((t >= 4) & (t < 10), 1, 0)
        sib = jnp.where((t >= 1) & (t < 7), 1, 0)

        @pl.when(t == 1)
        def _():
            arrive([c_copy(i) for i in range(8)])

        @pl.when(t == 2)
        def _():
            for r in range(NY):
                for sign in (1, -1):
                    z_copy(3, sign, r).wait_recv()
                    if r in halves(4, 4, sign):
                        z_copy(4, sign, r).start()
            arrive([s_copy(3, 1), s_copy(3, -1)])
            s_copy(4, 1).start()

        @pl.when(t == 4)
        def _():
            arrive([z_copy(4, sign, r) for sign in (1, -1) for r in halves(4, 4, sign)])
            s_copy(4, 1).wait_recv()
            join(range(4, 8))
            send_dq(2, 0)

        cols = pl.ds(pl.multiple_of(late * (4 * CH), 4 * CH), 4 * CH)
        js = pl.ds(pl.multiple_of(sib * HALF, HALF), HALF)
        norms = stat_all[pl.ds(h, 1), cols]
        dels = stat_all[pl.ds(8 + h, 1), cols]
        rows_q = qg[h, cols]
        both = kv[h, js]
        zero = jnp.zeros_like(both)
        scores = nt(jnp.where(lane < D, both, zero), rows_q)
        dweights = nt(jnp.where(lane < D, zero, both), rows_q)
        weights = jnp.exp(scores - norms)
        dscores = (weights * (dweights - dels)).astype(BF16)
        low = weights.astype(BF16)
        dkv[h, js] += jnp.where(lane < D, nn(dscores, rows_q), nn(low, rows_q))
        dqt[h, :, cols] += tn(both, dscores)[:D]

        @pl.when((t >= 4) & (t < 7))
        def _():
            send_core(h)

        @pl.when((t >= 7) & (t < 10))
        def _():
            send_dq(h, 1)

        @pl.when(t >= 9)
        def _():
            send_x(h)

        @pl.when(t >= 10)
        def _():
            send_dq(h, 0)

    def fkv_copy(h, r):
        return remote(
            fin_kv.at[h, pl.ds(r * SUB, SUB)], r_kv.at[h, y], f_send.at[h, r], f_recv.at[h, r],
            dev(dy=r),
        )

    def fq_copy(r):
        return remote(fin_q.at[r], r_fq.at[y], f_send.at[HL, r], f_recv.at[HL, r], dev(dy=r))

    for h in (2, 0, 1):
        arrive([kx_copy(h, d) for d in X_SLOT if d])
        total = dkv[h, :CH]
        for slot in range(NX - 1):
            total = total + r_x[h, slot].astype(F32)
        total = total.astype(BF16)
        fin_kv[h] = total
        start([fkv_copy(h, r) for r in order])
        r_kv[h, y] = total[:SUB]
    for h in range(HL):
        arrive([q_copy(h, d) for d in Z_SLOT if d])
        total = dq16[h, 0].astype(F32)
        for slot in range(1, NZ):
            total = total + r_q[h, slot].astype(F32)
        total = total.astype(BF16)
        for r in range(NY):
            at = (r % 2) * SUB
            side = (r // 2) * D
            fin_q[r, :, h * D : (h + 1) * D] = total[at : at + SUB, side : side + D]
    start([fq_copy(r) for r in order])
    r_fq[y] = fin_q[0]
    arrive([fkv_copy(h, r) for h in range(HL) for r in order] + [fq_copy(r) for r in order])
    out_kv[...] = r_kv[...]
    out_q[...] = r_fq[...]

    done = [y_copy(r, kind) for r in order for kind in range(3)]
    for step in range(1, NZ // 2 + 1):
        for sign in (1, -1):
            done += [z_copy(step, sign, r) for r in halves(step, NZ // 2, sign)]
            if step < NZ // 2 or sign > 0:
                done.append(s_copy(step, sign))
    for step in range(1, NX // 2 + 1):
        for sign in (1, -1):
            done += [x_copy(step, sign, r) for r in halves(step, NX // 2, sign)]
    done += [c_copy(i) for i in range(8)] + [kc_copy(h) for h in range(HL)]
    done += [kx_copy(h, d) for h in range(HL) for d in X_SLOT if d]
    done += [q_copy(h, d) for h in range(HL) for d in Z_SLOT if d]
    done += [fkv_copy(h, r) for h in range(HL) for r in order] + [fq_copy(r) for r in order]
    for copy in done:
        copy.wait_send()
    for score in range(2):

        @pl.when(jnp.logical_not(lse_local(score)))
        def _():
            lse_copy(score).wait_send()


def place(kv_ref, q_ref, dq_ref, dk_ref, dv_ref):
    for n in range(NY):
        for h in range(HL):
            cols = slice((n * HL + h) * D, (n * HL + h + 1) * D)
            pair = kv_ref[h, n]
            dk_ref[:, cols] = pair[:, :D]
            dv_ref[:, cols] = pair[:, D:]
        dq_ref[:, n * HL * D : (n + 1) * HL * D] = q_ref[n]


def local(queries, keys, values, attended, grad_out, logsumexp):
    dma = pltpu.SemaphoreType.DMA
    vm = pltpu.VMEM
    whole = pl.BlockSpec(memory_space=pltpu.VMEM)
    sums = pl.pallas_call(
        kernel,
        out_shape=(
            jax.ShapeDtypeStruct((HL, NY, SUB, 2 * D), BF16),
            jax.ShapeDtypeStruct((NY, SUB, HL * D), BF16),
        ),
        in_specs=[whole] * 6,
        out_specs=[whole] * 2,
        scratch_shapes=[
            vm((NY, HL, SUB, 2 * D), BF16),
            vm((NY, HL, SUB, 2 * D), BF16),
            vm((NY, 8, SUB), F32),
            vm((2, 2, 8, SUB), F32),
            vm((HL, NI, 2 * D), BF16),
            vm((HL, NJ, 2 * D), BF16),
            vm((2, 2, 8, SUB), F32),
            vm((NY, 8, SUB), F32),
            vm((NZ, 16, CH), F32),
            vm((16, NI), F32),
            vm((HL, D, NI), F32),
            vm((HL, NJ, 2 * D), F32),
            vm((HL, HALF, 2 * D), BF16),
            vm((HL, HALF, 2 * D), BF16),
            vm((HL, HALF - CH, 2 * D), BF16),
            vm((HL, NX - 1, CH, 2 * D), BF16),
            vm((HL, NZ, PK, 2 * D), BF16),
            vm((HL, NZ, PK, 2 * D), BF16),
            vm((HL, CH, 2 * D), BF16),
            vm((NY, SUB, HL * D), BF16),
            vm((HL, NY, SUB, 2 * D), BF16),
            vm((NY, SUB, HL * D), BF16),
            dma((NY, 3)), dma((NY, 3)),
            dma((2,)), dma((2,)),
            dma((2, NZ // 2 + 1, NY)), dma((2, NZ // 2 + 1, NY)),
            dma((2, NZ // 2 + 1)), dma((2, NZ // 2 + 1)),
            dma((2, NX // 2 + 1, NY)), dma((2, NX // 2 + 1, NY)),
            dma((8,)), dma((8,)),
            dma((HL,)), dma((HL,)),
            dma((HL, NX)), dma((HL, NX)),
            dma((HL, NZ)), dma((HL, NZ)),
            dma((HL + 1, NY)), dma((HL + 1, NY)),
        ],
        compiler_params=pltpu.CompilerParams(
            collective_id=0, has_side_effects=True, vmem_limit_bytes=56 << 20
        ),
        name="attention_grad",
    )(queries, keys, values, attended, grad_out, jnp.transpose(logsumexp))
    out = jax.ShapeDtypeStruct(queries.shape, BF16)
    return pl.pallas_call(
        place, out_shape=(out, out, out), in_specs=[whole] * 2, out_specs=[whole] * 3, name="place"
    )(*sums)


def solution(mesh):
    rows = P(("ctx", "head"), None)
    return jax.shard_map(
        local,
        mesh=mesh,
        in_specs=(rows,) * 5 + (P("ctx", "head"),),
        out_specs=(rows,) * 3,
        check_vma=False,
    )
```

```python
import functools

import jax
import jax.numpy as jnp
from jax import lax
from jax.experimental import pallas as pl
from jax.experimental.pallas import tpu as pltpu
from jax.sharding import PartitionSpec as P

F32 = jnp.float32
BF16 = jnp.bfloat16
MESH = pl.DeviceIdType.MESH

NX, NY, NZ = 4, 4, 8
HL = 3
D = 64
SUB = 48
CH = NY * SUB
NI = NZ * CH
NJ = 2 * NX * CH
HALF = NJ // 2
Z_SLOT = {0: 0, 1: 1, -1: 2, 2: 3, -2: 4, 3: 5, -3: 6, 4: 7}
X_SLOT = {0: 0, 1: 1, -1: 2, 2: 3}
NC = NY + 2 * (NX - 1)
PK = CH // 2


def nt(a, b):
    return lax.dot_general(a, b, (((1,), (1,)), ((), ())), preferred_element_type=F32)


def tn(a, b):
    return lax.dot_general(a, b, (((0,), (0,)), ((), ())), preferred_element_type=F32)


def nn(a, b):
    return jnp.dot(a, b, preferred_element_type=F32)


def kernel(
    q_ref, k_ref, v_ref, o_ref, g_ref, lse_ref, out_kv, out_q,
    st_qg, st_kv, st_d, st_lse, qg, kv, r_lse, r_d, stat, stat_all, dqt, dkv, dkv16, r_core, x16,
    r_x, dq32, dq16, r_v, r_q, fin_kv, fin_q, r_kv, r_fq,
    a_send, a_recv, l_send, l_recv, z_send, z_recv, s_send, s_recv, x_send, x_recv, c_send, c_recv,
    kc_send, kc_recv, kx_send, kx_recv, v_send, v_recv, q_send, q_recv, f_send, f_recv,
):
    c = lax.axis_index("ctx")
    g = lax.axis_index("head")
    z = c % NZ
    x = (c // NZ) % NX
    y_lo = c // (NZ * NX)
    y_hi = g // 2
    core = g % 2
    y = 2 * y_hi + y_lo

    def dev(dx=0, dy=0, dz=0, other=False):
        yy = (y + dy) % NY
        cc = (yy % 2) * (NX * NZ) + ((x + dx + NX) % NX) * NZ + (z + dz + NZ) % NZ
        return (cc, (yy // 2) * 2 + (1 - core if other else core))

    def remote(src, dst, send, recv, to):
        return pltpu.make_async_remote_copy(
            src_ref=src, dst_ref=dst, send_sem=send, recv_sem=recv, device_id=to,
            device_id_type=MESH,
        )

    def start(copies):
        for copy in copies:
            copy.start()

    def arrive(copies):
        for copy in copies:
            copy.wait_recv()

    barrier = pltpu.get_barrier_semaphore()
    peers = [dev(dy=dy, other=o) for dy in range(NY) for o in (False, True) if dy or o]
    peers += [dev(dz=d) for d in (1, -1, 2, -2)] + [dev(dx=d) for d in X_SLOT if d]
    for peer in peers:
        pl.semaphore_signal(barrier, inc=1, device_id=peer, device_id_type=MESH)

    def y_copy(r, kind):
        group = (y + r) % NY
        rows = pl.ds((NY - r) * SUB, SUB)
        src = (st_qg, st_kv, st_d)[kind].at[group]
        dst = (qg.at[:, rows], kv.at[:, rows], r_d.at[NY - r])[kind]
        return remote(src, dst, a_send.at[r, kind], a_recv.at[r, kind], dev(dy=r))

    def z_copy(step, sign, r):
        d = -sign * (step - 1)
        a = Z_SLOT[d]
        b = Z_SLOT[4 if step == NZ // 2 else d - sign]
        way = 0 if sign > 0 else 1
        return remote(
            qg.at[:, pl.ds(a * CH + r * SUB, SUB)], qg.at[:, pl.ds(b * CH + r * SUB, SUB)],
            z_send.at[way, step, r], z_recv.at[way, step, r], dev(dz=sign),
        )

    def x_copy(d, r):
        back = X_SLOT[2 if d == 2 else -d]
        return remote(
            kv.at[:, pl.ds(r * SUB, SUB)], kv.at[:, pl.ds(back * CH + r * SUB, SUB)],
            x_send.at[X_SLOT[d], r], x_recv.at[X_SLOT[d], r], dev(dx=d),
        )

    def x_copies(r):
        return [x_copy(d, r) for d in (2, 1, -1)]

    def parts(step, sign):
        return range(NY) if step < NZ // 2 else ((0, 1) if sign > 0 else (2, 3))

    def s_copy(step, sign):
        d = -sign * (step - 1)
        way = 0 if sign > 0 else 1
        return remote(
            stat.at[Z_SLOT[d]], stat.at[Z_SLOT[4 if step == NZ // 2 else d - sign]],
            s_send.at[way, step], s_recv.at[way, step], dev(dz=sign),
        )

    def c_copy(i):
        if i < NY:
            begin, rows = i * SUB, SUB
        else:
            begin, rows = CH + ((i - NY) // 2) * CH + (i % 2) * (CH // 2), CH // 2
        return remote(
            kv.at[:, pl.ds(begin, rows)], kv.at[:, pl.ds(HALF + begin, rows)],
            c_send.at[i], c_recv.at[i], dev(other=True),
        )

    lse_to = (g % 2) * (NX * NZ) + x * NZ + z
    lse_own = core == y_lo

    def lse_copy(score):
        return remote(
            st_lse.at[score], r_lse.at[y_lo], l_send.at[score], l_recv.at[y_lo],
            (lse_to, (g // 2) * 2 + score),
        )

    def lse_local(score):
        return lse_own & (core == score)

    def stage(st, left, right):
        for n in range(NY * HL):
            cols = slice(n * D, (n + 1) * D)
            st[n // HL, n % HL] = jnp.concatenate([left[:, cols], right[:, cols]], axis=1)

    order = (1, 3, 2)
    stage(st_kv, k_ref[...], v_ref[...])
    pl.semaphore_wait(barrier, len(peers))
    start([y_copy(r, 1) for r in order])
    kv[:, 0:SUB] = st_kv[y]
    start(x_copies(0) + [c_copy(0)])
    gs = g_ref[...]
    stage(st_qg, q_ref[...] * jnp.asarray(0.125, BF16), gs)
    start([y_copy(r, 0) for r in order])
    qg[:, 0:SUB] = st_qg[y]
    start([z_copy(1, 1, 0), z_copy(1, -1, 0)])
    prod = gs.astype(F32) * o_ref[...].astype(F32)
    hi = prod.astype(BF16)
    lo = (prod - hi.astype(F32)).astype(BF16)
    row = lax.broadcasted_iota(jnp.int32, (8 * NY, NY * HL * D), 0)
    col = lax.broadcasted_iota(jnp.int32, (8 * NY, NY * HL * D), 1)
    begin = ((row // 8) * HL + row % 8) * D
    pick = ((row % 8 < HL) & (col >= begin) & (col < begin + D)).astype(F32).astype(BF16)
    deltas = nt(pick, hi) + nt(pick, lo)
    for n in range(NY):
        st_d[n] = deltas[8 * n : 8 * n + 8]
    start([y_copy(r, 2) for r in order])
    st_lse[...] = jnp.zeros_like(st_lse)
    for s in range(NY):
        st_lse[s % 2, s // 2, 0:HL] = lse_ref[:, s * SUB : (s + 1) * SUB]
    for score in range(2):

        @pl.when(jnp.logical_not(lse_local(score)))
        def _():
            lse_copy(score).start()

        @pl.when(lse_local(score))
        def _():
            r_lse[y_lo] = st_lse[score]

    r_d[0] = st_d[y]
    dqt[...] = jnp.zeros_like(dqt)
    dkv[...] = jnp.zeros_like(dkv)

    for r, kind in ((1, 1), (3, 1), (1, 0), (3, 0), (2, 1), (2, 0)):
        y_copy(NY - r, kind).wait_recv()
        if kind == 1:
            start(x_copies(r) + [c_copy(r)])
        else:
            start([z_copy(1, 1, r), z_copy(1, -1, r)])
    for r in range(1, NY):
        y_copy(r, 2).wait_recv()
    for source in range(2):

        @pl.when(jnp.logical_not(lse_own & (source == y_lo)))
        def _():
            remote(
                st_lse.at[0], r_lse.at[source], l_send.at[0], l_recv.at[source],
                (lse_to, (g // 2) * 2),
            ).wait_recv()

    for r in range(NY):
        from_at = (y + r) % NY
        stat[0, 0:8, r * SUB : (r + 1) * SUB] = r_lse[from_at % 2, from_at // 2]
        stat[0, 8:16, r * SUB : (r + 1) * SUB] = r_d[r]
    start([s_copy(1, 1), s_copy(1, -1)])
    for i, r in enumerate((0, 1, 3, 2)):
        arrive(x_copies(r))
        if i % 2:
            start([c_copy(NY + 2 * n + i // 2) for n in range(NX - 1)])
        for sign in (1, -1):
            z_copy(1, sign, r).wait_recv()
            z_copy(2, sign, r).start()
    for sign in (1, -1):
        s_copy(1, sign).wait_recv()
        s_copy(2, sign).start()
    for r in (0, 1, 3, 2):
        for sign in (1, -1):
            z_copy(2, sign, r).wait_recv()
            z_copy(3, sign, r).start()
    for sign in (1, -1):
        s_copy(2, sign).wait_recv()
        s_copy(3, sign).start()

    def join(slots):
        for slot in slots:
            stat_all[:, slot * CH : (slot + 1) * CH] = stat[slot]

    join(range(4))

    def v_copy(h, i):
        slot = (5, 6, 7, 7)[i]
        rows = pl.ds((0, 0, 0, PK // 2)[i], (PK, PK, PK // 2, PK // 2)[i])
        return remote(
            dq16.at[h, slot, rows], r_v.at[h, i, rows], v_send.at[h, i], v_recv.at[h, i],
            dev(dz=(2, -2, 2, -2)[i]),
        )

    def q_copy(h, d):
        slot = Z_SLOT[d]
        back = Z_SLOT[-d]
        return remote(
            dq16.at[h, slot], r_q.at[h, back], q_send.at[h, slot], q_recv.at[h, slot], dev(dz=d)
        )

    def pack_dq(h, half):
        cols = slice(half * 4 * CH, (half + 1) * 4 * CH)
        block = jnp.transpose(dqt[h, :, cols]) * 0.125
        for t in range(4):
            piece = block[t * CH : (t + 1) * CH]
            dq32[h, 4 * half + t] = jnp.concatenate([piece[:PK], piece[PK:]], axis=1)

    def send_far(h):
        for slot in (5, 6, 7):
            dq16[h, slot] = dq32[h, slot].astype(BF16)
        start([v_copy(h, i) for i in range(4)])

    def send_near(h):
        arrive([v_copy(h, i) for i in range(4)])
        half = PK // 2
        dq16[h, 1] = (dq32[h, 1] + r_v[h, 0].astype(F32)).astype(BF16)
        dq16[h, 2] = (dq32[h, 2] + r_v[h, 1].astype(F32)).astype(BF16)
        dq16[h, 3, :half] = (dq32[h, 3, :half] + r_v[h, 2, :half].astype(F32)).astype(BF16)
        dq16[h, 3, half:] = dq32[h, 3, half:].astype(BF16)
        dq16[h, 4, :half] = dq32[h, 4, :half].astype(BF16)
        dq16[h, 4, half:] = (dq32[h, 4, half:] + r_v[h, 3, half:].astype(F32)).astype(BF16)
        start([q_copy(h, d) for d in (2, -2, 1, -1)])

    def kc_copy(h):
        return remote(dkv16.at[h], r_core.at[h], kc_send.at[h], kc_recv.at[h], dev(other=True))

    def send_core(h):
        dkv16[h] = dkv[h, HALF:].astype(BF16)
        kc_copy(h).start()

    def kx_copy(h, d):
        slot = X_SLOT[d]
        back = X_SLOT[2 if d == 2 else -d]
        return remote(
            x16.at[h, pl.ds((slot - 1) * CH, CH)], r_x.at[h, back - 1], kx_send.at[h, slot],
            kx_recv.at[h, slot], dev(dx=d),
        )

    def send_x(h):
        kc_copy(h).wait_recv()
        total = dkv[h, :HALF] + r_core[h].astype(F32)
        x16[h] = total[CH:].astype(BF16)
        start([kx_copy(h, d) for d in X_SLOT if d])
        dkv[h, :CH] = total[:CH]

    lane = lax.broadcasted_iota(jnp.int32, (HALF, 2 * D), 1)

    @pl.loop(0, 4 * HL)
    def _(t):
        h = jnp.where((t >= 7) & (t < 10), t + 1, t + 2) % HL
        late = jnp.where((t >= 4) & (t < 10), 1, 0)
        sib = jnp.where((t >= 1) & (t < 7), 1, 0)

        @pl.when(t == 1)
        def _():
            arrive([c_copy(i) for i in range(NC)])

        @pl.when(t == 2)
        def _():
            for r in range(NY):
                for sign in (1, -1):
                    z_copy(3, sign, r).wait_recv()
                    if r in parts(4, sign):
                        z_copy(4, sign, r).start()
            arrive([s_copy(3, 1), s_copy(3, -1)])
            s_copy(4, 1).start()

        @pl.when(t == 4)
        def _():
            arrive([z_copy(4, sign, r) for sign in (1, -1) for r in parts(4, sign)])
            s_copy(4, 1).wait_recv()
            join(range(4, 8))
            pack_dq(2, 0)

        cols = pl.ds(pl.multiple_of(late * (4 * CH), 4 * CH), 4 * CH)
        js = pl.ds(pl.multiple_of(sib * HALF, HALF), HALF)
        norms = stat_all[pl.ds(h, 1), cols]
        dels = stat_all[pl.ds(8 + h, 1), cols]
        rows_q = qg[h, cols]
        both = kv[h, js]
        zero = jnp.zeros_like(both)
        scores = nt(jnp.where(lane < D, both, zero), rows_q)
        dweights = nt(jnp.where(lane < D, zero, both), rows_q)
        weights = jnp.exp(scores - norms)
        dscores = (weights * (dweights - dels)).astype(BF16)
        low = weights.astype(BF16)
        dkv[h, js] += jnp.where(lane < D, nn(dscores, rows_q), nn(low, rows_q))
        dqt[h, :, cols] += tn(both, dscores)[:D]

        @pl.when((t >= 4) & (t < 7))
        def _():
            send_core(h)

        @pl.when((t >= 7) & (t < 10))
        def _():
            pack_dq(h, 1)
            send_far(h)

        @pl.when(t == 7)
        def _():
            send_x(2)

        @pl.when(t >= 10)
        def _():
            send_x(h)
            pack_dq(h, 0)

        @pl.when(t == 10)
        def _():
            send_near(2)

    send_near(0)
    send_near(1)

    def fkv_copy(h, r):
        return remote(
            fin_kv.at[h, pl.ds(r * SUB, SUB)], r_kv.at[h, y], f_send.at[h, r], f_recv.at[h, r],
            dev(dy=r),
        )

    def fq_copy(r):
        return remote(fin_q.at[r], r_fq.at[y], f_send.at[HL, r], f_recv.at[HL, r], dev(dy=r))

    for h in (2, 0, 1):
        arrive([kx_copy(h, d) for d in X_SLOT if d])
        total = dkv[h, :CH]
        for slot in range(NX - 1):
            total = total + r_x[h, slot].astype(F32)
        total = total.astype(BF16)
        fin_kv[h] = total
        start([fkv_copy(h, r) for r in order])
        r_kv[h, y] = total[:SUB]
    for h in (2, 0, 1):
        arrive([q_copy(h, d) for d in (2, -2, 1, -1)])
        total = dq32[h, 0]
        for slot in range(1, 5):
            total = total + r_q[h, slot].astype(F32)
        total = total.astype(BF16)
        for r in range(NY):
            at = (r % 2) * SUB
            side = (r // 2) * D
            fin_q[r, :, h * D : (h + 1) * D] = total[at : at + SUB, side : side + D]
    start([fq_copy(r) for r in order])
    r_fq[y] = fin_q[0]
    arrive([fkv_copy(h, r) for h in range(HL) for r in order] + [fq_copy(r) for r in order])
    out_kv[...] = r_kv[...]
    out_q[...] = r_fq[...]

    done = [y_copy(r, kind) for r in order for kind in range(3)]
    for step in range(1, NZ // 2 + 1):
        for sign in (1, -1):
            done += [z_copy(step, sign, r) for r in parts(step, sign)]
            if step < NZ // 2 or sign > 0:
                done.append(s_copy(step, sign))
    done += [copy for r in range(NY) for copy in x_copies(r)]
    done += [c_copy(i) for i in range(NC)] + [kc_copy(h) for h in range(HL)]
    done += [kx_copy(h, d) for h in range(HL) for d in X_SLOT if d]
    done += [q_copy(h, d) for h in range(HL) for d in (2, -2, 1, -1)]
    done += [v_copy(h, i) for h in range(HL) for i in range(4)]
    done += [fkv_copy(h, r) for h in range(HL) for r in order] + [fq_copy(r) for r in order]
    for copy in done:
        copy.wait_send()
    for score in range(2):

        @pl.when(jnp.logical_not(lse_local(score)))
        def _():
            lse_copy(score).wait_send()


def place(kv_ref, q_ref, dq_ref, dk_ref, dv_ref):
    for n in range(NY):
        for h in range(HL):
            cols = slice((n * HL + h) * D, (n * HL + h + 1) * D)
            pair = kv_ref[h, n]
            dk_ref[:, cols] = pair[:, :D]
            dv_ref[:, cols] = pair[:, D:]
        dq_ref[:, n * HL * D : (n + 1) * HL * D] = q_ref[n]


def local(queries, keys, values, attended, grad_out, logsumexp):
    dma = pltpu.SemaphoreType.DMA
    vm = pltpu.VMEM
    whole = pl.BlockSpec(memory_space=pltpu.VMEM)
    sums = pl.pallas_call(
        kernel,
        out_shape=(
            jax.ShapeDtypeStruct((HL, NY, SUB, 2 * D), BF16),
            jax.ShapeDtypeStruct((NY, SUB, HL * D), BF16),
        ),
        in_specs=[whole] * 6,
        out_specs=[whole] * 2,
        scratch_shapes=[
            vm((NY, HL, SUB, 2 * D), BF16),
            vm((NY, HL, SUB, 2 * D), BF16),
            vm((NY, 8, SUB), F32),
            vm((2, 2, 8, SUB), F32),
            vm((HL, NI, 2 * D), BF16),
            vm((HL, NJ, 2 * D), BF16),
            vm((2, 2, 8, SUB), F32),
            vm((NY, 8, SUB), F32),
            vm((NZ, 16, CH), F32),
            vm((16, NI), F32),
            vm((HL, D, NI), F32),
            vm((HL, NJ, 2 * D), F32),
            vm((HL, HALF, 2 * D), BF16),
            vm((HL, HALF, 2 * D), BF16),
            vm((HL, HALF - CH, 2 * D), BF16),
            vm((HL, NX - 1, CH, 2 * D), BF16),
            vm((HL, NZ, PK, 2 * D), F32),
            vm((HL, NZ, PK, 2 * D), BF16),
            vm((HL, 4, PK, 2 * D), BF16),
            vm((HL, 5, PK, 2 * D), BF16),
            vm((HL, CH, 2 * D), BF16),
            vm((NY, SUB, HL * D), BF16),
            vm((HL, NY, SUB, 2 * D), BF16),
            vm((NY, SUB, HL * D), BF16),
            dma((NY, 3)), dma((NY, 3)),
            dma((2,)), dma((2,)),
            dma((2, NZ // 2 + 1, NY)), dma((2, NZ // 2 + 1, NY)),
            dma((2, NZ // 2 + 1)), dma((2, NZ // 2 + 1)),
            dma((NX, NY)), dma((NX, NY)),
            dma((NC,)), dma((NC,)),
            dma((HL,)), dma((HL,)),
            dma((HL, NX)), dma((HL, NX)),
            dma((HL, 4)), dma((HL, 4)),
            dma((HL, 5)), dma((HL, 5)),
            dma((HL + 1, NY)), dma((HL + 1, NY)),
        ],
        compiler_params=pltpu.CompilerParams(
            collective_id=0, has_side_effects=True, vmem_limit_bytes=56 << 20
        ),
        name="attention_grad",
    )(queries, keys, values, attended, grad_out, jnp.transpose(logsumexp))
    out = jax.ShapeDtypeStruct(queries.shape, BF16)
    return pl.pallas_call(
        place, out_shape=(out, out, out), in_specs=[whole] * 2, out_specs=[whole] * 3, name="place"
    )(*sums)


def solution(mesh):
    rows = P(("ctx", "head"), None)
    return jax.shard_map(
        local,
        mesh=mesh,
        in_specs=(rows,) * 5 + (P("ctx", "head"),),
        out_specs=(rows,) * 3,
        check_vma=False,
    )
```

```python
import functools

import jax
import jax.numpy as jnp
from jax import lax
from jax.experimental import pallas as pl
from jax.experimental.pallas import tpu as pltpu
from jax.sharding import PartitionSpec as P

F32 = jnp.float32
BF16 = jnp.bfloat16
MESH = pl.DeviceIdType.MESH

NX, NY, NZ = 4, 4, 8
HL = 3
D = 64
SUB = 48
CH = NY * SUB
NI = NZ * CH
NJ = 2 * NX * CH
HALF = NJ // 2
Z_SLOT = {0: 0, 1: 1, -1: 2, 2: 3, -2: 4, 3: 5, -3: 6, 4: 7}
X_SLOT = {0: 0, 1: 1, -1: 2, 2: 3}
NC = NY + 2 * (NX - 1)
PK = CH // 2


def nt(a, b):
    return lax.dot_general(a, b, (((1,), (1,)), ((), ())), preferred_element_type=F32)


def tn(a, b):
    return lax.dot_general(a, b, (((0,), (0,)), ((), ())), preferred_element_type=F32)


def nn(a, b):
    return jnp.dot(a, b, preferred_element_type=F32)


def kernel(
    q_ref, k_ref, v_ref, o_ref, g_ref, lse_ref, out_kv, out_q,
    st_qg, st_kv, st_d, st_lse, qg, kv, r_lse, r_d, stat, stat_all, dqt, dkv, dkv16, r_core, x16,
    r_x, dq32, dq16, r_v, r_q, fin_kv, fin_q, r_kv, r_fq,
    a_send, a_recv, l_send, l_recv, z_send, z_recv, s_send, s_recv, x_send, x_recv, c_send, c_recv,
    kc_send, kc_recv, kx_send, kx_recv, v_send, v_recv, q_send, q_recv, f_send, f_recv,
):
    c = lax.axis_index("ctx")
    g = lax.axis_index("head")
    z = c % NZ
    x = (c // NZ) % NX
    y_lo = c // (NZ * NX)
    y_hi = g // 2
    core = g % 2
    y = 2 * y_hi + y_lo

    def dev(dx=0, dy=0, dz=0, other=False):
        yy = (y + dy) % NY
        cc = (yy % 2) * (NX * NZ) + ((x + dx + NX) % NX) * NZ + (z + dz + NZ) % NZ
        return (cc, (yy // 2) * 2 + (1 - core if other else core))

    def remote(src, dst, send, recv, to):
        return pltpu.make_async_remote_copy(
            src_ref=src, dst_ref=dst, send_sem=send, recv_sem=recv, device_id=to,
            device_id_type=MESH,
        )

    def start(copies):
        for copy in copies:
            copy.start()

    def arrive(copies):
        for copy in copies:
            copy.wait_recv()

    barrier = pltpu.get_barrier_semaphore()
    peers = [dev(dy=dy, other=o) for dy in range(NY) for o in (False, True) if dy or o]
    peers += [dev(dz=d) for d in (1, -1, 2, -2)] + [dev(dx=d) for d in X_SLOT if d]
    for peer in peers:
        pl.semaphore_signal(barrier, inc=1, device_id=peer, device_id_type=MESH)

    def y_copy(r, kind):
        group = (y + r) % NY
        rows = pl.ds((NY - r) * SUB, SUB)
        src = (st_qg, st_kv, st_d)[kind].at[group]
        dst = (qg.at[:, rows], kv.at[:, rows], r_d.at[NY - r])[kind]
        return remote(src, dst, a_send.at[r, kind], a_recv.at[r, kind], dev(dy=r))

    def z_copy(step, sign, r):
        d = -sign * (step - 1)
        a = Z_SLOT[d]
        b = Z_SLOT[4 if step == NZ // 2 else d - sign]
        way = 0 if sign > 0 else 1
        return remote(
            qg.at[:, pl.ds(a * CH + r * SUB, SUB)], qg.at[:, pl.ds(b * CH + r * SUB, SUB)],
            z_send.at[way, step, r], z_recv.at[way, step, r], dev(dz=sign),
        )

    def x_copy(d, r):
        back = X_SLOT[2 if d == 2 else -d]
        return remote(
            kv.at[:, pl.ds(r * SUB, SUB)], kv.at[:, pl.ds(back * CH + r * SUB, SUB)],
            x_send.at[X_SLOT[d], r], x_recv.at[X_SLOT[d], r], dev(dx=d),
        )

    def x_copies(r):
        return [x_copy(d, r) for d in (2, 1, -1)]

    def parts(step, sign):
        return range(NY) if step < NZ // 2 else ((0, 1) if sign > 0 else (2, 3))

    def s_copy(step, sign):
        d = -sign * (step - 1)
        way = 0 if sign > 0 else 1
        return remote(
            stat.at[Z_SLOT[d]], stat.at[Z_SLOT[4 if step == NZ // 2 else d - sign]],
            s_send.at[way, step], s_recv.at[way, step], dev(dz=sign),
        )

    def c_copy(i):
        if i < NY:
            begin, rows = i * SUB, SUB
        else:
            begin, rows = CH + ((i - NY) // 2) * CH + (i % 2) * (CH // 2), CH // 2
        return remote(
            kv.at[:, pl.ds(begin, rows)], kv.at[:, pl.ds(HALF + begin, rows)],
            c_send.at[i], c_recv.at[i], dev(other=True),
        )

    lse_to = (g % 2) * (NX * NZ) + x * NZ + z
    lse_own = core == y_lo

    def lse_copy(score):
        return remote(
            st_lse.at[score], r_lse.at[y_lo], l_send.at[score], l_recv.at[y_lo],
            (lse_to, (g // 2) * 2 + score),
        )

    def lse_local(score):
        return lse_own & (core == score)

    def stage(st, left, right):
        for n in range(NY * HL):
            cols = slice(n * D, (n + 1) * D)
            st[n // HL, n % HL] = jnp.concatenate([left[:, cols], right[:, cols]], axis=1)

    order = (1, 3, 2)
    stage(st_kv, k_ref[...], v_ref[...])
    pl.semaphore_wait(barrier, len(peers))
    start([y_copy(r, 1) for r in order])
    kv[:, 0:SUB] = st_kv[y]
    start(x_copies(0) + [c_copy(0)])
    gs = g_ref[...]
    stage(st_qg, q_ref[...] * jnp.asarray(0.125, BF16), gs)
    start([y_copy(r, 0) for r in order])
    qg[:, 0:SUB] = st_qg[y]
    start([z_copy(1, 1, 0), z_copy(1, -1, 0)])
    prod = gs.astype(F32) * o_ref[...].astype(F32)
    hi = prod.astype(BF16)
    lo = (prod - hi.astype(F32)).astype(BF16)
    row = lax.broadcasted_iota(jnp.int32, (8 * NY, NY * HL * D), 0)
    col = lax.broadcasted_iota(jnp.int32, (8 * NY, NY * HL * D), 1)
    begin = ((row // 8) * HL + row % 8) * D
    pick = ((row % 8 < HL) & (col >= begin) & (col < begin + D)).astype(F32).astype(BF16)
    deltas = nt(pick, hi) + nt(pick, lo)
    for n in range(NY):
        st_d[n] = deltas[8 * n : 8 * n + 8]
    start([y_copy(r, 2) for r in order])
    st_lse[...] = jnp.zeros_like(st_lse)
    for s in range(NY):
        st_lse[s % 2, s // 2, 0:HL] = lse_ref[:, s * SUB : (s + 1) * SUB]
    for score in range(2):

        @pl.when(jnp.logical_not(lse_local(score)))
        def _():
            lse_copy(score).start()

        @pl.when(lse_local(score))
        def _():
            r_lse[y_lo] = st_lse[score]

    r_d[0] = st_d[y]
    dqt[...] = jnp.zeros_like(dqt)
    dkv[...] = jnp.zeros_like(dkv)

    for r, kind in ((1, 1), (3, 1), (1, 0), (3, 0), (2, 1), (2, 0)):
        y_copy(NY - r, kind).wait_recv()
        if kind == 1:
            start(x_copies(r) + [c_copy(r)])
        else:
            start([z_copy(1, 1, r), z_copy(1, -1, r)])
    for r in range(1, NY):
        y_copy(r, 2).wait_recv()
    for source in range(2):

        @pl.when(jnp.logical_not(lse_own & (source == y_lo)))
        def _():
            remote(
                st_lse.at[0], r_lse.at[source], l_send.at[0], l_recv.at[source],
                (lse_to, (g // 2) * 2),
            ).wait_recv()

    for r in range(NY):
        from_at = (y + r) % NY
        stat[0, 0:8, r * SUB : (r + 1) * SUB] = r_lse[from_at % 2, from_at // 2]
        stat[0, 8:16, r * SUB : (r + 1) * SUB] = r_d[r]
    start([s_copy(1, 1), s_copy(1, -1)])
    for i, r in enumerate((0, 1, 3, 2)):
        arrive(x_copies(r))
        if i % 2:
            start([c_copy(NY + 2 * n + i // 2) for n in range(NX - 1)])
        for sign in (1, -1):
            z_copy(1, sign, r).wait_recv()
            z_copy(2, sign, r).start()
    for sign in (1, -1):
        s_copy(1, sign).wait_recv()
        s_copy(2, sign).start()
    for r in (0, 1, 3, 2):
        for sign in (1, -1):
            z_copy(2, sign, r).wait_recv()
            z_copy(3, sign, r).start()
    for sign in (1, -1):
        s_copy(2, sign).wait_recv()
        s_copy(3, sign).start()

    def join(slots):
        for slot in slots:
            stat_all[:, slot * CH : (slot + 1) * CH] = stat[slot]

    join(range(4))

    def v_copy(h, i):
        slot = (5, 6, 7, 7)[i]
        rows = pl.ds((0, 0, 0, PK // 2)[i], (PK, PK, PK // 2, PK // 2)[i])
        return remote(
            dq16.at[h, slot, rows], r_v.at[h, i, rows], v_send.at[h, i], v_recv.at[h, i],
            dev(dz=(2, -2, 2, -2)[i]),
        )

    def q_copy(h, d):
        slot = Z_SLOT[d]
        back = Z_SLOT[-d]
        return remote(
            dq16.at[h, slot], r_q.at[h, back], q_send.at[h, slot], q_recv.at[h, slot], dev(dz=d)
        )

    def pack_dq(h, half):
        cols = slice(half * 4 * CH, (half + 1) * 4 * CH)
        block = jnp.transpose(dqt[h, :, cols]) * 0.125
        for t in range(4):
            piece = block[t * CH : (t + 1) * CH]
            dq32[h, 4 * half + t] = jnp.concatenate([piece[:PK], piece[PK:]], axis=1)

    def send_far(h):
        for slot in (5, 6, 7):
            dq16[h, slot] = dq32[h, slot].astype(BF16)
        start([v_copy(h, i) for i in range(4)])

    def send_near(h):
        arrive([v_copy(h, i) for i in range(4)])
        half = PK // 2
        dq16[h, 1] = (dq32[h, 1] + r_v[h, 0].astype(F32)).astype(BF16)
        dq16[h, 2] = (dq32[h, 2] + r_v[h, 1].astype(F32)).astype(BF16)
        dq16[h, 3, :half] = (dq32[h, 3, :half] + r_v[h, 2, :half].astype(F32)).astype(BF16)
        dq16[h, 3, half:] = dq32[h, 3, half:].astype(BF16)
        dq16[h, 4, :half] = dq32[h, 4, :half].astype(BF16)
        dq16[h, 4, half:] = (dq32[h, 4, half:] + r_v[h, 3, half:].astype(F32)).astype(BF16)
        start([q_copy(h, d) for d in (2, -2, 1, -1)])

    def kc_copy(h):
        return remote(dkv16.at[h], r_core.at[h], kc_send.at[h], kc_recv.at[h], dev(other=True))

    def send_core(h):
        dkv16[h] = dkv[h, HALF:].astype(BF16)
        kc_copy(h).start()

    def kx_copy(h, d):
        slot = X_SLOT[d]
        back = X_SLOT[2 if d == 2 else -d]
        return remote(
            x16.at[h, pl.ds((slot - 1) * CH, CH)], r_x.at[h, back - 1], kx_send.at[h, slot],
            kx_recv.at[h, slot], dev(dx=d),
        )

    def send_x(h):
        kc_copy(h).wait_recv()
        total = dkv[h, :HALF] + r_core[h].astype(F32)
        x16[h] = total[CH:].astype(BF16)
        start([kx_copy(h, d) for d in X_SLOT if d])
        dkv[h, :CH] = total[:CH]

    def fkv_copy(h, r):
        return remote(
            fin_kv.at[h, pl.ds(r * SUB, SUB)], r_kv.at[h, y], f_send.at[h, r], f_recv.at[h, r],
            dev(dy=r),
        )

    def fq_copy(r):
        return remote(fin_q.at[r], r_fq.at[y], f_send.at[HL, r], f_recv.at[HL, r], dev(dy=r))

    def finish_kv(h):
        arrive([kx_copy(h, d) for d in X_SLOT if d])
        total = dkv[h, :CH]
        for slot in range(NX - 1):
            total = total + r_x[h, slot].astype(F32)
        total = total.astype(BF16)
        fin_kv[h] = total
        start([fkv_copy(h, r) for r in order])
        r_kv[h, y] = total[:SUB]

    def finish_q(h):
        arrive([q_copy(h, d) for d in (2, -2, 1, -1)])
        total = dq32[h, 0]
        for slot in range(1, 5):
            total = total + r_q[h, slot].astype(F32)
        total = total.astype(BF16)
        for r in range(NY):
            at = (r % 2) * SUB
            side = (r // 2) * D
            fin_q[r, :, h * D : (h + 1) * D] = total[at : at + SUB, side : side + D]

    lane = lax.broadcasted_iota(jnp.int32, (HALF, 2 * D), 1)

    @pl.loop(0, 4 * HL)
    def _(t):
        h = jnp.where(t < 4, t % 2, (t - 4) // 2)
        h = jnp.where(t < 8, h, 2)
        late = jnp.where((t >= 4) & (t < 10), 1, 0)
        sib = jnp.where((t == 3) | ((t >= 2) & (t % 2 == 0)), 1, 0)

        @pl.when(t == 2)
        def _():
            arrive([c_copy(i) for i in range(NC)])
            for r in range(NY):
                for sign in (1, -1):
                    z_copy(3, sign, r).wait_recv()
                    if r in parts(4, sign):
                        z_copy(4, sign, r).start()
            arrive([s_copy(3, 1), s_copy(3, -1)])
            s_copy(4, 1).start()

        @pl.when(t == 4)
        def _():
            arrive([z_copy(4, sign, r) for sign in (1, -1) for r in parts(4, sign)])
            s_copy(4, 1).wait_recv()
            join(range(4, 8))

        cols = pl.ds(pl.multiple_of(late * (4 * CH), 4 * CH), 4 * CH)
        js = pl.ds(pl.multiple_of(sib * HALF, HALF), HALF)
        norms = stat_all[pl.ds(h, 1), cols]
        dels = stat_all[pl.ds(8 + h, 1), cols]
        rows_q = qg[h, cols]
        both = kv[h, js]
        zero = jnp.zeros_like(both)
        scores = nt(jnp.where(lane < D, both, zero), rows_q)
        dweights = nt(jnp.where(lane < D, zero, both), rows_q)
        weights = jnp.exp(scores - norms)
        dscores = (weights * (dweights - dels)).astype(BF16)
        low = weights.astype(BF16)
        dkv[h, js] += jnp.where(lane < D, nn(dscores, rows_q), nn(low, rows_q))
        dqt[h, :, cols] += tn(both, dscores)[:D]

        @pl.when((t == 2) | (t == 3) | (t == 11))
        def _():
            pack_dq(h, 0)

        @pl.when((t == 4) | (t == 6) | (t == 10))
        def _():
            send_core(h)

        @pl.when((t == 5) | (t == 7) | (t == 9))
        def _():
            pack_dq(h, 1)
            send_far(h)

        @pl.when((t == 5) | (t == 7) | (t == 11))
        def _():
            send_x(h)

        @pl.when((t == 8) | (t == 10))
        def _():
            send_near((t - 8) // 2)
            finish_kv((t - 8) // 2)

        @pl.when(t == 10)
        def _():
            finish_q(0)

    send_near(2)
    finish_q(1)
    finish_kv(2)
    finish_q(2)
    start([fq_copy(r) for r in order])
    r_fq[y] = fin_q[0]
    arrive([fkv_copy(h, r) for h in range(HL) for r in order] + [fq_copy(r) for r in order])
    out_kv[...] = r_kv[...]
    out_q[...] = r_fq[...]

    done = [y_copy(r, kind) for r in order for kind in range(3)]
    for step in range(1, NZ // 2 + 1):
        for sign in (1, -1):
            done += [z_copy(step, sign, r) for r in parts(step, sign)]
            if step < NZ // 2 or sign > 0:
                done.append(s_copy(step, sign))
    done += [copy for r in range(NY) for copy in x_copies(r)]
    done += [c_copy(i) for i in range(NC)] + [kc_copy(h) for h in range(HL)]
    done += [kx_copy(h, d) for h in range(HL) for d in X_SLOT if d]
    done += [q_copy(h, d) for h in range(HL) for d in (2, -2, 1, -1)]
    done += [v_copy(h, i) for h in range(HL) for i in range(4)]
    done += [fkv_copy(h, r) for h in range(HL) for r in order] + [fq_copy(r) for r in order]
    for copy in done:
        copy.wait_send()
    for score in range(2):

        @pl.when(jnp.logical_not(lse_local(score)))
        def _():
            lse_copy(score).wait_send()


def place(kv_ref, q_ref, dq_ref, dk_ref, dv_ref):
    for n in range(NY):
        for h in range(HL):
            cols = slice((n * HL + h) * D, (n * HL + h + 1) * D)
            pair = kv_ref[h, n]
            dk_ref[:, cols] = pair[:, :D]
            dv_ref[:, cols] = pair[:, D:]
        dq_ref[:, n * HL * D : (n + 1) * HL * D] = q_ref[n]


def local(queries, keys, values, attended, grad_out, logsumexp):
    dma = pltpu.SemaphoreType.DMA
    vm = pltpu.VMEM
    whole = pl.BlockSpec(memory_space=pltpu.VMEM)
    sums = pl.pallas_call(
        kernel,
        out_shape=(
            pltpu.VMEM((HL, NY, SUB, 2 * D), BF16),
            pltpu.VMEM((NY, SUB, HL * D), BF16),
        ),
        in_specs=[whole] * 6,
        out_specs=[whole] * 2,
        scratch_shapes=[
            vm((NY, HL, SUB, 2 * D), BF16),
            vm((NY, HL, SUB, 2 * D), BF16),
            vm((NY, 8, SUB), F32),
            vm((2, 2, 8, SUB), F32),
            vm((HL, NI, 2 * D), BF16),
            vm((HL, NJ, 2 * D), BF16),
            vm((2, 2, 8, SUB), F32),
            vm((NY, 8, SUB), F32),
            vm((NZ, 16, CH), F32),
            vm((16, NI), F32),
            vm((HL, D, NI), F32),
            vm((HL, NJ, 2 * D), F32),
            vm((HL, HALF, 2 * D), BF16),
            vm((HL, HALF, 2 * D), BF16),
            vm((HL, HALF - CH, 2 * D), BF16),
            vm((HL, NX - 1, CH, 2 * D), BF16),
            vm((HL, NZ, PK, 2 * D), F32),
            vm((HL, NZ, PK, 2 * D), BF16),
            vm((HL, 4, PK, 2 * D), BF16),
            vm((HL, 5, PK, 2 * D), BF16),
            vm((HL, CH, 2 * D), BF16),
            vm((NY, SUB, HL * D), BF16),
            vm((HL, NY, SUB, 2 * D), BF16),
            vm((NY, SUB, HL * D), BF16),
            dma((NY, 3)), dma((NY, 3)),
            dma((2,)), dma((2,)),
            dma((2, NZ // 2 + 1, NY)), dma((2, NZ // 2 + 1, NY)),
            dma((2, NZ // 2 + 1)), dma((2, NZ // 2 + 1)),
            dma((NX, NY)), dma((NX, NY)),
            dma((NC,)), dma((NC,)),
            dma((HL,)), dma((HL,)),
            dma((HL, NX)), dma((HL, NX)),
            dma((HL, 4)), dma((HL, 4)),
            dma((HL, 5)), dma((HL, 5)),
            dma((HL + 1, NY)), dma((HL + 1, NY)),
        ],
        compiler_params=pltpu.CompilerParams(
            collective_id=0, has_side_effects=True, vmem_limit_bytes=56 << 20
        ),
        name="attention_grad",
    )(queries, keys, values, attended, grad_out, jnp.transpose(logsumexp))
    out = jax.ShapeDtypeStruct(queries.shape, BF16)
    return pl.pallas_call(
        place, out_shape=(out, out, out), in_specs=[whole] * 2, out_specs=[whole] * 3, name="place"
    )(*[pltpu.with_memory_space_constraint(part, pltpu.VMEM) for part in sums])


def solution(mesh):
    rows = P(("ctx", "head"), None)
    return jax.shard_map(
        local,
        mesh=mesh,
        in_specs=(rows,) * 5 + (P("ctx", "head"),),
        out_specs=(rows,) * 3,
        check_vma=False,
    )
```

```python
import functools

import jax
import jax.numpy as jnp
from jax import lax
from jax.experimental import pallas as pl
from jax.experimental.pallas import tpu as pltpu
from jax.sharding import PartitionSpec as P

F32 = jnp.float32
BF16 = jnp.bfloat16
MESH = pl.DeviceIdType.MESH

NX, NY, NZ = 4, 4, 8
HL = 3
D = 64
SUB = 48
CH = NY * SUB
NI = NZ * CH
NJ = 2 * NX * CH
HALF = NJ // 2
Z_SLOT = {0: 0, 1: 1, -1: 2, 2: 3, -2: 4, 3: 5, -3: 6, 4: 7}
X_SLOT = {0: 0, 1: 1, -1: 2, 2: 3}
NC = NY + 2 * (NX - 1)
HS = SUB // 2
PK = CH // 2


def nt(a, b):
    return lax.dot_general(a, b, (((1,), (1,)), ((), ())), preferred_element_type=F32)


def tn(a, b):
    return lax.dot_general(a, b, (((0,), (0,)), ((), ())), preferred_element_type=F32)


def nn(a, b):
    return jnp.dot(a, b, preferred_element_type=F32)


def kernel(
    q_ref, k_ref, v_ref, o_ref, g_ref, lse_ref, out_kv, out_q,
    st_qg, st_kv, st_d, st_lse, qg, kv, r_lse, r_d, stat, stat_all, dqt, dkv, dkv16, r_core, x16,
    r_x, dq32, dq16, r_v, r_q, fin_kv, fin_q, r_kv, r_fq, last_kv, r_lkv, last_q, r_lq,
    a_send, a_recv, l_send, l_recv, z_send, z_recv, s_send, s_recv, x_send, x_recv, c_send, c_recv,
    kc_send, kc_recv, kx_send, kx_recv, v_send, v_recv, q_send, q_recv, f_send, f_recv,
    lx_send, lx_recv, lq_send, lq_recv,
):
    c = lax.axis_index("ctx")
    g = lax.axis_index("head")
    z = c % NZ
    x = (c // NZ) % NX
    y_lo = c // (NZ * NX)
    y_hi = g // 2
    core = g % 2
    y = 2 * y_hi + y_lo

    def dev(dx=0, dy=0, dz=0, other=False):
        yy = (y + dy) % NY
        cc = (yy % 2) * (NX * NZ) + ((x + dx + NX) % NX) * NZ + (z + dz + NZ) % NZ
        return (cc, (yy // 2) * 2 + (1 - core if other else core))

    def remote(src, dst, send, recv, to):
        return pltpu.make_async_remote_copy(
            src_ref=src, dst_ref=dst, send_sem=send, recv_sem=recv, device_id=to,
            device_id_type=MESH,
        )

    def start(copies):
        for copy in copies:
            copy.start()

    def arrive(copies):
        for copy in copies:
            copy.wait_recv()

    barrier = pltpu.get_barrier_semaphore()
    peers = [dev(dy=dy, other=o) for dy in range(NY) for o in (False, True) if dy or o]
    peers += [dev(dz=d) for d in (1, -1, 2, -2)] + [dev(dx=d) for d in X_SLOT if d]
    for peer in peers:
        pl.semaphore_signal(barrier, inc=1, device_id=peer, device_id_type=MESH)

    def y_copy(r, kind):
        group = (y + r) % NY
        rows = pl.ds((NY - r) * SUB, SUB)
        src = (st_qg, st_kv, st_d)[kind].at[group]
        dst = (qg.at[:, rows], kv.at[:, rows], r_d.at[NY - r])[kind]
        return remote(src, dst, a_send.at[r, kind], a_recv.at[r, kind], dev(dy=r))

    def z_copy(step, sign, r):
        d = -sign * (step - 1)
        a = Z_SLOT[d]
        b = Z_SLOT[4 if step == NZ // 2 else d - sign]
        way = 0 if sign > 0 else 1
        return remote(
            qg.at[:, pl.ds(a * CH + r * SUB, SUB)], qg.at[:, pl.ds(b * CH + r * SUB, SUB)],
            z_send.at[way, step, r], z_recv.at[way, step, r], dev(dz=sign),
        )

    def x_copy(d, r):
        back = X_SLOT[2 if d == 2 else -d]
        return remote(
            kv.at[:, pl.ds(r * SUB, SUB)], kv.at[:, pl.ds(back * CH + r * SUB, SUB)],
            x_send.at[X_SLOT[d], r], x_recv.at[X_SLOT[d], r], dev(dx=d),
        )

    def x_copies(r):
        return [x_copy(d, r) for d in (2, 1, -1)]

    def parts(step, sign):
        return range(NY) if step < NZ // 2 else ((0, 1) if sign > 0 else (2, 3))

    def s_copy(step, sign):
        d = -sign * (step - 1)
        way = 0 if sign > 0 else 1
        return remote(
            stat.at[Z_SLOT[d]], stat.at[Z_SLOT[4 if step == NZ // 2 else d - sign]],
            s_send.at[way, step], s_recv.at[way, step], dev(dz=sign),
        )

    def c_copy(i):
        if i < NY:
            begin, rows = i * SUB, SUB
        else:
            begin, rows = CH + ((i - NY) // 2) * CH + (i % 2) * (CH // 2), CH // 2
        return remote(
            kv.at[:, pl.ds(begin, rows)], kv.at[:, pl.ds(HALF + begin, rows)],
            c_send.at[i], c_recv.at[i], dev(other=True),
        )

    lse_to = (g % 2) * (NX * NZ) + x * NZ + z
    lse_own = core == y_lo

    def lse_copy(score):
        return remote(
            st_lse.at[score], r_lse.at[y_lo], l_send.at[score], l_recv.at[y_lo],
            (lse_to, (g // 2) * 2 + score),
        )

    def lse_local(score):
        return lse_own & (core == score)

    def stage(st, left, right):
        for n in range(NY * HL):
            cols = slice(n * D, (n + 1) * D)
            st[n // HL, n % HL] = jnp.concatenate([left[:, cols], right[:, cols]], axis=1)

    order = (1, 3, 2)
    stage(st_kv, k_ref[...], v_ref[...])
    pl.semaphore_wait(barrier, len(peers))
    start([y_copy(r, 1) for r in order])
    kv[:, 0:SUB] = st_kv[y]
    start(x_copies(0) + [c_copy(0)])
    gs = g_ref[...]
    stage(st_qg, q_ref[...] * jnp.asarray(0.125, BF16), gs)
    start([y_copy(r, 0) for r in order])
    qg[:, 0:SUB] = st_qg[y]
    start([z_copy(1, 1, 0), z_copy(1, -1, 0)])
    prod = gs.astype(F32) * o_ref[...].astype(F32)
    hi = prod.astype(BF16)
    lo = (prod - hi.astype(F32)).astype(BF16)
    row = lax.broadcasted_iota(jnp.int32, (8 * NY, NY * HL * D), 0)
    col = lax.broadcasted_iota(jnp.int32, (8 * NY, NY * HL * D), 1)
    begin = ((row // 8) * HL + row % 8) * D
    pick = ((row % 8 < HL) & (col >= begin) & (col < begin + D)).astype(F32).astype(BF16)
    deltas = nt(pick, hi) + nt(pick, lo)
    for n in range(NY):
        st_d[n] = deltas[8 * n : 8 * n + 8]
    start([y_copy(r, 2) for r in order])
    st_lse[...] = jnp.zeros_like(st_lse)
    for s in range(NY):
        st_lse[s % 2, s // 2, 0:HL] = lse_ref[:, s * SUB : (s + 1) * SUB]
    for score in range(2):

        @pl.when(jnp.logical_not(lse_local(score)))
        def _():
            lse_copy(score).start()

        @pl.when(lse_local(score))
        def _():
            r_lse[y_lo] = st_lse[score]

    r_d[0] = st_d[y]
    dqt[...] = jnp.zeros_like(dqt)
    dkv[...] = jnp.zeros_like(dkv)

    for r, kind in ((1, 1), (3, 1), (1, 0), (3, 0), (2, 1), (2, 0)):
        y_copy(NY - r, kind).wait_recv()
        if kind == 1:
            start(x_copies(r) + [c_copy(r)])
        else:
            start([z_copy(1, 1, r), z_copy(1, -1, r)])
    for r in range(1, NY):
        y_copy(r, 2).wait_recv()
    for source in range(2):

        @pl.when(jnp.logical_not(lse_own & (source == y_lo)))
        def _():
            remote(
                st_lse.at[0], r_lse.at[source], l_send.at[0], l_recv.at[source],
                (lse_to, (g // 2) * 2),
            ).wait_recv()

    for r in range(NY):
        from_at = (y + r) % NY
        stat[0, 0:8, r * SUB : (r + 1) * SUB] = r_lse[from_at % 2, from_at // 2]
        stat[0, 8:16, r * SUB : (r + 1) * SUB] = r_d[r]
    start([s_copy(1, 1), s_copy(1, -1)])
    for i, r in enumerate((0, 1, 3, 2)):
        arrive(x_copies(r))
        if i % 2:
            start([c_copy(NY + 2 * n + i // 2) for n in range(NX - 1)])
        for sign in (1, -1):
            z_copy(1, sign, r).wait_recv()
            z_copy(2, sign, r).start()
    for sign in (1, -1):
        s_copy(1, sign).wait_recv()
        s_copy(2, sign).start()
    for r in (0, 1, 3, 2):
        for sign in (1, -1):
            z_copy(2, sign, r).wait_recv()
            z_copy(3, sign, r).start()
    for sign in (1, -1):
        s_copy(2, sign).wait_recv()
        s_copy(3, sign).start()

    def join(slots):
        for slot in slots:
            stat_all[:, slot * CH : (slot + 1) * CH] = stat[slot]

    join(range(4))

    def v_copy(h, i):
        slot = (5, 6, 7, 7)[i]
        rows = pl.ds((0, 0, 0, PK // 2)[i], (PK, PK, PK // 2, PK // 2)[i])
        return remote(
            dq16.at[h, slot, rows], r_v.at[h, i, rows], v_send.at[h, i], v_recv.at[h, i],
            dev(dz=(2, -2, 2, -2)[i]),
        )

    def q_copy(h, d):
        slot = Z_SLOT[d]
        back = Z_SLOT[-d]
        return remote(
            dq16.at[h, slot], r_q.at[h, back], q_send.at[h, slot], q_recv.at[h, slot], dev(dz=d)
        )

    def pack_dq(h, half):
        cols = slice(half * 4 * CH, (half + 1) * 4 * CH)
        block = jnp.transpose(dqt[h, :, cols]) * 0.125
        for t in range(4):
            for r in range(NY):
                at = t * CH + r * SUB
                dq32[h, 4 * half + t, r * HS : (r + 1) * HS] = jnp.concatenate(
                    [block[at : at + HS], block[at + HS : at + SUB]], axis=1
                )

    def send_far(h):
        for slot in (5, 6, 7):
            dq16[h, slot] = dq32[h, slot].astype(BF16)
        start([v_copy(h, i) for i in range(4)])

    def add_near(h):
        arrive([v_copy(h, i) for i in range(4)])
        half = PK // 2
        dq16[h, 1] = (dq32[h, 1] + r_v[h, 0].astype(F32)).astype(BF16)
        dq16[h, 2] = (dq32[h, 2] + r_v[h, 1].astype(F32)).astype(BF16)
        dq16[h, 3, :half] = (dq32[h, 3, :half] + r_v[h, 2, :half].astype(F32)).astype(BF16)
        dq16[h, 3, half:] = dq32[h, 3, half:].astype(BF16)
        dq16[h, 4, :half] = dq32[h, 4, :half].astype(BF16)
        dq16[h, 4, half:] = (dq32[h, 4, half:] + r_v[h, 3, half:].astype(F32)).astype(BF16)

    def send_near(h):
        add_near(h)
        start([q_copy(h, d) for d in (2, -2, 1, -1)])

    NEAR = (2, -2, 1, -1, 0)
    FAR_X = (2, 1, -1, 0)

    def lq_copy(d, r):
        slot = Z_SLOT[d]
        return remote(
            last_q.at[slot, r], r_lq.at[y, Z_SLOT[-d]], lq_send.at[slot, r], lq_recv.at[slot, r],
            dev(dz=d, dy=r),
        )

    def lx_copy(d, r):
        slot = X_SLOT[d]
        back = X_SLOT[2 if d == 2 else -d]
        return remote(
            last_kv.at[pl.ds(slot * CH + r * SUB, SUB)], r_lkv.at[y, back], lx_send.at[slot, r],
            lx_recv.at[slot, r], dev(dx=d, dy=r),
        )

    last_x = [lx_copy(d, r) for r in (2, 1, 3, 0) for d in FAR_X if d or r]
    last_z = [lq_copy(d, r) for r in (2, 1, 3, 0) for d in NEAR if d or r]

    def kc_copy(h):
        return remote(dkv16.at[h], r_core.at[h], kc_send.at[h], kc_recv.at[h], dev(other=True))

    def send_core(h):
        dkv16[h] = dkv[h, HALF:].astype(BF16)
        kc_copy(h).start()

    def kx_copy(h, d):
        slot = X_SLOT[d]
        back = X_SLOT[2 if d == 2 else -d]
        return remote(
            x16.at[h, pl.ds((slot - 1) * CH, CH)], r_x.at[h, back - 1], kx_send.at[h, slot],
            kx_recv.at[h, slot], dev(dx=d),
        )

    def all_cores(h):
        kc_copy(h).wait_recv()
        return dkv[h, :HALF] + r_core[h].astype(F32)

    def send_x(h):
        total = all_cores(h)
        x16[h] = total[CH:].astype(BF16)
        start([kx_copy(h, d) for d in X_SLOT if d])
        dkv[h, :CH] = total[:CH]

    def fkv_copy(h, r):
        return remote(
            fin_kv.at[h, pl.ds(r * SUB, SUB)], r_kv.at[h, y], f_send.at[h, r], f_recv.at[h, r],
            dev(dy=r),
        )

    def fq_copy(r):
        return remote(fin_q.at[r], r_fq.at[y], f_send.at[HL - 1, r], f_recv.at[HL - 1, r], dev(dy=r))

    def finish_kv(h):
        arrive([kx_copy(h, d) for d in X_SLOT if d])
        total = dkv[h, :CH]
        for slot in range(NX - 1):
            total = total + r_x[h, slot].astype(F32)
        total = total.astype(BF16)
        fin_kv[h] = total
        start([fkv_copy(h, r) for r in order])
        r_kv[h, y] = total[:SUB]

    def unpack(rows):
        return jnp.concatenate([rows[:, :D], rows[:, D:]], axis=0).astype(BF16)

    def finish_q(h):
        arrive([q_copy(h, d) for d in (2, -2, 1, -1)])
        total = dq32[h, 0]
        for slot in range(1, 5):
            total = total + r_q[h, slot].astype(F32)
        for r in range(NY):
            fin_q[r, :, h * D : (h + 1) * D] = unpack(total[r * HS : (r + 1) * HS])

    lane = lax.broadcasted_iota(jnp.int32, (HALF, 2 * D), 1)

    @pl.loop(0, 4 * HL)
    def _(t):
        h = jnp.where(t < 4, t % 2, (t - 4) // 2)
        h = jnp.where(t < 8, h, 2)
        late = jnp.where((t >= 4) & (t < 10), 1, 0)
        sib = jnp.where((t == 3) | ((t >= 2) & (t % 2 == 0)), 1, 0)

        @pl.when(t == 2)
        def _():
            arrive([c_copy(i) for i in range(NC)])
            for r in range(NY):
                for sign in (1, -1):
                    z_copy(3, sign, r).wait_recv()
                    if r in parts(4, sign):
                        z_copy(4, sign, r).start()
            arrive([s_copy(3, 1), s_copy(3, -1)])
            s_copy(4, 1).start()

        @pl.when(t == 4)
        def _():
            arrive([z_copy(4, sign, r) for sign in (1, -1) for r in parts(4, sign)])
            s_copy(4, 1).wait_recv()
            join(range(4, 8))

        cols = pl.ds(pl.multiple_of(late * (4 * CH), 4 * CH), 4 * CH)
        js = pl.ds(pl.multiple_of(sib * HALF, HALF), HALF)
        norms = stat_all[pl.ds(h, 1), cols]
        dels = stat_all[pl.ds(8 + h, 1), cols]
        rows_q = qg[h, cols]
        both = kv[h, js]
        zero = jnp.zeros_like(both)
        scores = nt(jnp.where(lane < D, both, zero), rows_q)
        dweights = nt(jnp.where(lane < D, zero, both), rows_q)
        weights = jnp.exp(scores - norms)
        dscores = (weights * (dweights - dels)).astype(BF16)
        low = weights.astype(BF16)
        dkv[h, js] += jnp.where(lane < D, nn(dscores, rows_q), nn(low, rows_q))
        dqt[h, :, cols] += tn(both, dscores)[:D]

        @pl.when((t == 2) | (t == 3))
        def _():
            pack_dq(h, 0)

        @pl.when((t == 4) | (t == 6) | (t == 10))
        def _():
            send_core(h)

        @pl.when((t == 5) | (t == 7) | (t == 9))
        def _():
            pack_dq(h, 1)
            send_far(h)

        @pl.when((t == 5) | (t == 7))
        def _():
            send_x(h)

        @pl.when((t == 8) | (t == 10))
        def _():
            send_near((t - 8) // 2)
            finish_kv((t - 8) // 2)

        @pl.when(t == 10)
        def _():
            finish_q(0)

    last = HL - 1
    last_kv[...] = all_cores(last).astype(BF16)
    start(last_x)
    r_lkv[y, 0] = last_kv[:SUB]
    pack_dq(last, 0)
    add_near(last)
    for r in range(NY):
        rows = slice(r * HS, (r + 1) * HS)
        last_q[0, r] = dq32[last, 0, rows].astype(BF16)
        for slot in range(1, 5):
            last_q[slot, r] = dq16[last, slot, rows]
    start(last_z)
    r_lq[y, 0] = last_q[0, 0]
    finish_q(1)
    start([fq_copy(r) for r in order])
    r_fq[y] = fin_q[0]
    arrive(last_x)
    for n in range(NY):
        total = r_lkv[n, 0].astype(F32)
        for slot in range(1, NX):
            total = total + r_lkv[n, slot].astype(F32)
        out_kv[last, n] = total.astype(BF16)
    arrive(last_z)
    for n in range(NY):
        total = r_lq[n, 0].astype(F32)
        for slot in range(1, 5):
            total = total + r_lq[n, slot].astype(F32)
        out_q[n, :, last * D : HL * D] = unpack(total)
    arrive([fkv_copy(h, r) for h in range(last) for r in order] + [fq_copy(r) for r in order])
    for h in range(last):
        out_kv[h] = r_kv[h]
    out_q[:, :, : last * D] = r_fq[...]

    done = [y_copy(r, kind) for r in order for kind in range(3)]
    for step in range(1, NZ // 2 + 1):
        for sign in (1, -1):
            done += [z_copy(step, sign, r) for r in parts(step, sign)]
            if step < NZ // 2 or sign > 0:
                done.append(s_copy(step, sign))
    done += [copy for r in range(NY) for copy in x_copies(r)]
    done += [c_copy(i) for i in range(NC)] + [kc_copy(h) for h in range(HL)]
    done += [kx_copy(h, d) for h in range(last) for d in X_SLOT if d]
    done += [q_copy(h, d) for h in range(last) for d in (2, -2, 1, -1)] + last_x + last_z
    done += [v_copy(h, i) for h in range(HL) for i in range(4)]
    done += [fkv_copy(h, r) for h in range(last) for r in order] + [fq_copy(r) for r in order]
    for copy in done:
        copy.wait_send()
    for score in range(2):

        @pl.when(jnp.logical_not(lse_local(score)))
        def _():
            lse_copy(score).wait_send()


def place(kv_ref, q_ref, dq_ref, dk_ref, dv_ref):
    for n in range(NY):
        for h in range(HL):
            cols = slice((n * HL + h) * D, (n * HL + h + 1) * D)
            pair = kv_ref[h, n]
            dk_ref[:, cols] = pair[:, :D]
            dv_ref[:, cols] = pair[:, D:]
        dq_ref[:, n * HL * D : (n + 1) * HL * D] = q_ref[n]


def local(queries, keys, values, attended, grad_out, logsumexp):
    dma = pltpu.SemaphoreType.DMA
    vm = pltpu.VMEM
    whole = pl.BlockSpec(memory_space=pltpu.VMEM)
    sums = pl.pallas_call(
        kernel,
        out_shape=(
            pltpu.VMEM((HL, NY, SUB, 2 * D), BF16),
            pltpu.VMEM((NY, SUB, HL * D), BF16),
        ),
        in_specs=[whole] * 6,
        out_specs=[whole] * 2,
        scratch_shapes=[
            vm((NY, HL, SUB, 2 * D), BF16),
            vm((NY, HL, SUB, 2 * D), BF16),
            vm((NY, 8, SUB), F32),
            vm((2, 2, 8, SUB), F32),
            vm((HL, NI, 2 * D), BF16),
            vm((HL, NJ, 2 * D), BF16),
            vm((2, 2, 8, SUB), F32),
            vm((NY, 8, SUB), F32),
            vm((NZ, 16, CH), F32),
            vm((16, NI), F32),
            vm((HL, D, NI), F32),
            vm((HL, NJ, 2 * D), F32),
            vm((HL, HALF, 2 * D), BF16),
            vm((HL, HALF, 2 * D), BF16),
            vm((HL, HALF - CH, 2 * D), BF16),
            vm((HL, NX - 1, CH, 2 * D), BF16),
            vm((HL, NZ, PK, 2 * D), F32),
            vm((HL, NZ, PK, 2 * D), BF16),
            vm((HL, 4, PK, 2 * D), BF16),
            vm((HL, 5, PK, 2 * D), BF16),
            vm((HL, CH, 2 * D), BF16),
            vm((NY, SUB, 2 * D), BF16),
            vm((HL - 1, NY, SUB, 2 * D), BF16),
            vm((NY, SUB, 2 * D), BF16),
            vm((HALF, 2 * D), BF16),
            vm((NY, NX, SUB, 2 * D), BF16),
            vm((5, NY, HS, 2 * D), BF16),
            vm((NY, 5, HS, 2 * D), BF16),
            dma((NY, 3)), dma((NY, 3)),
            dma((2,)), dma((2,)),
            dma((2, NZ // 2 + 1, NY)), dma((2, NZ // 2 + 1, NY)),
            dma((2, NZ // 2 + 1)), dma((2, NZ // 2 + 1)),
            dma((NX, NY)), dma((NX, NY)),
            dma((NC,)), dma((NC,)),
            dma((HL,)), dma((HL,)),
            dma((HL, NX)), dma((HL, NX)),
            dma((HL, 4)), dma((HL, 4)),
            dma((HL, 5)), dma((HL, 5)),
            dma((HL, NY)), dma((HL, NY)),
            dma((NX, NY)), dma((NX, NY)),
            dma((5, NY)), dma((5, NY)),
        ],
        compiler_params=pltpu.CompilerParams(
            collective_id=0, has_side_effects=True, vmem_limit_bytes=56 << 20
        ),
        name="attention_grad",
    )(queries, keys, values, attended, grad_out, jnp.transpose(logsumexp))
    out = jax.ShapeDtypeStruct(queries.shape, BF16)
    return pl.pallas_call(
        place, out_shape=(out, out, out), in_specs=[whole] * 2, out_specs=[whole] * 3, name="place"
    )(*[pltpu.with_memory_space_constraint(part, pltpu.VMEM) for part in sums])


def solution(mesh):
    rows = P(("ctx", "head"), None)
    return jax.shard_map(
        local,
        mesh=mesh,
        in_specs=(rows,) * 5 + (P("ctx", "head"),),
        out_specs=(rows,) * 3,
        check_vma=False,
    )
```

```python
import functools

import jax
import jax.numpy as jnp
from jax import lax
from jax.experimental import pallas as pl
from jax.experimental.pallas import tpu as pltpu
from jax.sharding import PartitionSpec as P

F32 = jnp.float32
BF16 = jnp.bfloat16
MESH = pl.DeviceIdType.MESH

NX, NY, NZ = 4, 4, 8
HL = 3
D = 64
SUB = 48
CH = NY * SUB
NI = NZ * CH
NJ = 2 * NX * CH
HALF = NJ // 2
Z_SLOT = {0: 0, 1: 1, -1: 2, 2: 3, -2: 4, 3: 5, -3: 6, 4: 7}
X_SLOT = {0: 0, 1: 1, -1: 2, 2: 3}
NC = NY + 2 * (NX - 1)
HS = SUB // 2
PK = CH // 2


def nt(a, b):
    return lax.dot_general(a, b, (((1,), (1,)), ((), ())), preferred_element_type=F32)


def tn(a, b):
    return lax.dot_general(a, b, (((0,), (0,)), ((), ())), preferred_element_type=F32)


def nn(a, b):
    return jnp.dot(a, b, preferred_element_type=F32)


def kernel(
    q_ref, k_ref, v_ref, o_ref, g_ref, lse_ref, out_kv, out_q,
    st_qg, st_kv, st_d, st_lse, qg, kv, pair, r_lse, r_d, stat, stat_all, dqt, dkv, dkv16, r_core, x16,
    r_x, dq32, dq16, r_v, r_q, fin_kv, fin_q, r_kv, r_fq, last_kv, r_lkv, last_q, r_lq,
    a_send, a_recv, l_send, l_recv, z_send, z_recv, s_send, s_recv, x_send, x_recv, c_send, c_recv,
    kc_send, kc_recv, kx_send, kx_recv, v_send, v_recv, q_send, q_recv, f_send, f_recv,
    lx_send, lx_recv, lq_send, lq_recv,
):
    c = lax.axis_index("ctx")
    g = lax.axis_index("head")
    z = c % NZ
    x = (c // NZ) % NX
    y_lo = c // (NZ * NX)
    y_hi = g // 2
    core = g % 2
    y = 2 * y_hi + y_lo

    def dev(dx=0, dy=0, dz=0, other=False):
        yy = (y + dy) % NY
        cc = (yy % 2) * (NX * NZ) + ((x + dx + NX) % NX) * NZ + (z + dz + NZ) % NZ
        return (cc, (yy // 2) * 2 + (1 - core if other else core))

    def remote(src, dst, send, recv, to):
        return pltpu.make_async_remote_copy(
            src_ref=src, dst_ref=dst, send_sem=send, recv_sem=recv, device_id=to,
            device_id_type=MESH,
        )

    def start(copies):
        for copy in copies:
            copy.start()

    def arrive(copies):
        for copy in copies:
            copy.wait_recv()

    barrier = pltpu.get_barrier_semaphore()
    peers = [dev(dy=dy) for dy in range(1, NY)] + [dev(other=True), dev(dz=1), dev(dz=-1)]
    peers += [dev(dx=d) for d in X_SLOT if d]
    for peer in peers:
        pl.semaphore_signal(barrier, inc=1, device_id=peer, device_id_type=MESH)

    def y_copy(r, kind):
        group = (y + r) % NY
        rows = pl.ds((NY - r) * SUB, SUB)
        src = (st_qg, st_kv, st_d)[kind].at[group]
        dst = (qg.at[:, rows], kv.at[:, rows], r_d.at[NY - r])[kind]
        return remote(src, dst, a_send.at[r, kind], a_recv.at[r, kind], dev(dy=r))

    def z_copy(step, sign, r):
        d = -sign * (step - 1)
        a = Z_SLOT[d]
        b = Z_SLOT[4 if step == NZ // 2 else d - sign]
        way = 0 if sign > 0 else 1
        return remote(
            qg.at[:, pl.ds(a * CH + r * SUB, SUB)], qg.at[:, pl.ds(b * CH + r * SUB, SUB)],
            z_send.at[way, step, r], z_recv.at[way, step, r], dev(dz=sign),
        )

    def x_copy(d, r):
        back = X_SLOT[2 if d == 2 else -d]
        return remote(
            kv.at[:, pl.ds(r * SUB, SUB)], kv.at[:, pl.ds(back * CH + r * SUB, SUB)],
            x_send.at[X_SLOT[d], r], x_recv.at[X_SLOT[d], r], dev(dx=d),
        )

    def x_copies(r):
        return [x_copy(d, r) for d in (2, 1, -1)]

    def parts(step, sign):
        return range(NY) if step < NZ // 2 else ((0, 1) if sign > 0 else (2, 3))

    def s_copy(step, sign):
        d = -sign * (step - 1)
        way = 0 if sign > 0 else 1
        return remote(
            stat.at[Z_SLOT[d]], stat.at[Z_SLOT[4 if step == NZ // 2 else d - sign]],
            s_send.at[way, step], s_recv.at[way, step], dev(dz=sign),
        )

    def c_copy(i):
        if i < NY:
            begin, rows = i * SUB, SUB
        else:
            begin, rows = CH + ((i - NY) // 2) * CH + (i % 2) * (CH // 2), CH // 2
        return remote(
            kv.at[:, pl.ds(begin, rows)], kv.at[:, pl.ds(HALF + begin, rows)],
            c_send.at[i], c_recv.at[i], dev(other=True),
        )

    def lse_core():
        return remote(
            st_lse.at[1 - core], pair.at[core], l_send.at[0], l_recv.at[0], dev(other=True)
        )

    def lse_y():
        there = (1 - y_lo) * (NX * NZ) + x * NZ + z
        return remote(pair.at[1 - y_lo], r_lse.at[y_lo], l_send.at[1], l_recv.at[1], (there, g))

    def stage(st, left, right):
        for n in range(NY * HL):
            cols = slice(n * D, (n + 1) * D)
            st[n // HL, n % HL] = jnp.concatenate([left[:, cols], right[:, cols]], axis=1)

    order = (1, 3, 2)
    stage(st_kv, k_ref[...], v_ref[...])
    pl.semaphore_wait(barrier, len(peers))
    start([y_copy(r, 1) for r in order])
    st_lse[...] = jnp.zeros_like(st_lse)
    for s in range(NY):
        st_lse[s % 2, s // 2, 0:HL] = lse_ref[:, s * SUB : (s + 1) * SUB]
    lse_core().start()
    pair[core] = st_lse[core]
    kv[:, 0:SUB] = st_kv[y]
    start(x_copies(0) + [c_copy(0)])
    gs = g_ref[...]
    stage(st_qg, q_ref[...] * jnp.asarray(0.125, BF16), gs)
    start([y_copy(r, 0) for r in order])
    qg[:, 0:SUB] = st_qg[y]
    start([z_copy(1, 1, 0), z_copy(1, -1, 0)])
    prod = gs.astype(F32) * o_ref[...].astype(F32)
    hi = prod.astype(BF16)
    lo = (prod - hi.astype(F32)).astype(BF16)
    row = lax.broadcasted_iota(jnp.int32, (8 * NY, NY * HL * D), 0)
    col = lax.broadcasted_iota(jnp.int32, (8 * NY, NY * HL * D), 1)
    begin = ((row // 8) * HL + row % 8) * D
    pick = ((row % 8 < HL) & (col >= begin) & (col < begin + D)).astype(F32).astype(BF16)
    deltas = nt(pick, hi) + nt(pick, lo)
    for n in range(NY):
        st_d[n] = deltas[8 * n : 8 * n + 8]
    start([y_copy(r, 2) for r in order])
    r_d[0] = st_d[y]
    dqt[...] = jnp.zeros_like(dqt)
    dkv[...] = jnp.zeros_like(dkv)
    lse_core().wait_recv()
    lse_y().start()
    r_lse[y_lo] = pair[y_lo]

    for r, kind in ((1, 1), (3, 1), (1, 0), (3, 0), (2, 1), (2, 0)):
        y_copy(NY - r, kind).wait_recv()
        if kind == 1:
            start(x_copies(r) + [c_copy(r)])
        else:
            start([z_copy(1, 1, r), z_copy(1, -1, r)])
    for r in range(1, NY):
        y_copy(r, 2).wait_recv()
    lse_y().wait_recv()
    for r in range(NY):
        from_at = (y + r) % NY
        both = jnp.concatenate([r_lse[from_at % 2, from_at // 2][:HL], r_d[r][: 8 - HL]], axis=0)
        stat[0, :, r * SUB : (r + 1) * SUB] = both
    start([s_copy(1, 1), s_copy(1, -1)])
    for i, r in enumerate((0, 1, 3, 2)):
        arrive(x_copies(r))
        if i % 2:
            start([c_copy(NY + 2 * n + i // 2) for n in range(NX - 1)])
        for sign in (1, -1):
            z_copy(1, sign, r).wait_recv()
            z_copy(2, sign, r).start()
    for sign in (1, -1):
        s_copy(1, sign).wait_recv()
        s_copy(2, sign).start()
    for r in (0, 1, 3, 2):
        for sign in (1, -1):
            z_copy(2, sign, r).wait_recv()
            z_copy(3, sign, r).start()
    for sign in (1, -1):
        s_copy(2, sign).wait_recv()
        s_copy(3, sign).start()

    def join(slots):
        for slot in slots:
            stat_all[:, slot * CH : (slot + 1) * CH] = stat[slot]

    join(range(4))

    def v_copy(h, i):
        slot = (5, 6, 7, 7)[i]
        rows = pl.ds((0, 0, 0, PK // 2)[i], (PK, PK, PK // 2, PK // 2)[i])
        return remote(
            dq16.at[h, slot, rows], r_v.at[h, i, rows], v_send.at[h, i], v_recv.at[h, i],
            dev(dz=(2, -2, 2, -2)[i]),
        )

    def q_copy(h, d):
        slot = Z_SLOT[d]
        back = Z_SLOT[-d]
        return remote(
            dq16.at[h, slot], r_q.at[h, back], q_send.at[h, slot], q_recv.at[h, slot], dev(dz=d)
        )

    def pack_dq(h, half):
        cols = slice(half * 4 * CH, (half + 1) * 4 * CH)
        block = jnp.transpose(dqt[h, :, cols]) * 0.125
        for t in range(4):
            for r in range(NY):
                at = t * CH + r * SUB
                dq32[h, 4 * half + t, r * HS : (r + 1) * HS] = jnp.concatenate(
                    [block[at : at + HS], block[at + HS : at + SUB]], axis=1
                )

    def send_far(h):
        for slot in (5, 6, 7):
            dq16[h, slot] = dq32[h, slot].astype(BF16)
        start([v_copy(h, i) for i in range(4)])

    def add_near(h):
        arrive([v_copy(h, i) for i in range(4)])
        half = PK // 2
        dq16[h, 1] = (dq32[h, 1] + r_v[h, 0].astype(F32)).astype(BF16)
        dq16[h, 2] = (dq32[h, 2] + r_v[h, 1].astype(F32)).astype(BF16)
        dq16[h, 3, :half] = (dq32[h, 3, :half] + r_v[h, 2, :half].astype(F32)).astype(BF16)
        dq16[h, 3, half:] = dq32[h, 3, half:].astype(BF16)
        dq16[h, 4, :half] = dq32[h, 4, :half].astype(BF16)
        dq16[h, 4, half:] = (dq32[h, 4, half:] + r_v[h, 3, half:].astype(F32)).astype(BF16)

    def send_near(h):
        add_near(h)
        start([q_copy(h, d) for d in (2, -2, 1, -1)])

    NEAR = (2, -2, 1, -1, 0)
    FAR_X = (2, 1, -1, 0)

    def lq_copy(d, r):
        slot = Z_SLOT[d]
        return remote(
            last_q.at[slot, r], r_lq.at[y, Z_SLOT[-d]], lq_send.at[slot, r], lq_recv.at[slot, r],
            dev(dz=d, dy=r),
        )

    def lx_copy(d, r):
        slot = X_SLOT[d]
        back = X_SLOT[2 if d == 2 else -d]
        return remote(
            last_kv.at[pl.ds(slot * CH + r * SUB, SUB)], r_lkv.at[y, back], lx_send.at[slot, r],
            lx_recv.at[slot, r], dev(dx=d, dy=r),
        )

    last_x = [lx_copy(d, r) for r in (2, 1, 3, 0) for d in FAR_X if d or r]
    last_z = [lq_copy(d, r) for r in (2, 1, 3, 0) for d in NEAR if d or r]

    def kc_copy(h):
        return remote(dkv16.at[h], r_core.at[h], kc_send.at[h], kc_recv.at[h], dev(other=True))

    def send_core(h):
        dkv16[h] = dkv[h, HALF:].astype(BF16)
        kc_copy(h).start()

    def kx_copy(h, d):
        slot = X_SLOT[d]
        back = X_SLOT[2 if d == 2 else -d]
        return remote(
            x16.at[h, pl.ds((slot - 1) * CH, CH)], r_x.at[h, back - 1], kx_send.at[h, slot],
            kx_recv.at[h, slot], dev(dx=d),
        )

    def all_cores(h):
        kc_copy(h).wait_recv()
        return dkv[h, :HALF] + r_core[h].astype(F32)

    def send_x(h):
        total = all_cores(h)
        x16[h] = total[CH:].astype(BF16)
        start([kx_copy(h, d) for d in X_SLOT if d])
        dkv[h, :CH] = total[:CH]

    def fkv_copy(h, r):
        return remote(
            fin_kv.at[h, pl.ds(r * SUB, SUB)], r_kv.at[h, y], f_send.at[h, r], f_recv.at[h, r],
            dev(dy=r),
        )

    def fq_copy(r):
        return remote(fin_q.at[r], r_fq.at[y], f_send.at[HL - 1, r], f_recv.at[HL - 1, r], dev(dy=r))

    def finish_kv(h):
        arrive([kx_copy(h, d) for d in X_SLOT if d])
        total = dkv[h, :CH]
        for slot in range(NX - 1):
            total = total + r_x[h, slot].astype(F32)
        total = total.astype(BF16)
        fin_kv[h] = total
        start([fkv_copy(h, r) for r in order])
        r_kv[h, y] = total[:SUB]

    def unpack(rows):
        return jnp.concatenate([rows[:, :D], rows[:, D:]], axis=0).astype(BF16)

    def finish_q(h):
        arrive([q_copy(h, d) for d in (2, -2, 1, -1)])
        total = dq32[h, 0]
        for slot in range(1, 5):
            total = total + r_q[h, slot].astype(F32)
        for r in range(NY):
            fin_q[r, :, h * D : (h + 1) * D] = unpack(total[r * HS : (r + 1) * HS])

    lane = lax.broadcasted_iota(jnp.int32, (HALF, 2 * D), 1)

    @pl.loop(0, 4 * HL)
    def _(t):
        h = jnp.where(t < 4, t % 2, (t - 4) // 2)
        h = jnp.where(t < 8, h, 2)
        late = jnp.where((t >= 4) & (t < 10), 1, 0)
        sib = jnp.where((t == 3) | ((t >= 2) & (t % 2 == 0)), 1, 0)

        @pl.when(t == 2)
        def _():
            arrive([c_copy(i) for i in range(NC)])
            for r in range(NY):
                for sign in (1, -1):
                    z_copy(3, sign, r).wait_recv()
                    if r in parts(4, sign):
                        z_copy(4, sign, r).start()
            arrive([s_copy(3, 1), s_copy(3, -1)])
            s_copy(4, 1).start()

        @pl.when(t == 4)
        def _():
            arrive([z_copy(4, sign, r) for sign in (1, -1) for r in parts(4, sign)])
            s_copy(4, 1).wait_recv()
            join(range(4, 8))

        cols = pl.ds(pl.multiple_of(late * (4 * CH), 4 * CH), 4 * CH)
        js = pl.ds(pl.multiple_of(sib * HALF, HALF), HALF)
        norms = stat_all[pl.ds(h, 1), cols]
        dels = stat_all[pl.ds(HL + h, 1), cols]
        rows_q = qg[h, cols]
        both = kv[h, js]
        zero = jnp.zeros_like(both)
        scores = nt(jnp.where(lane < D, both, zero), rows_q)
        dweights = nt(jnp.where(lane < D, zero, both), rows_q)
        weights = jnp.exp(scores - norms)
        dscores = (weights * (dweights - dels)).astype(BF16)
        low = weights.astype(BF16)
        dkv[h, js] += jnp.where(lane < D, nn(dscores, rows_q), nn(low, rows_q))
        dqt[h, :, cols] += tn(both, dscores)[:D]

        @pl.when((t == 2) | (t == 3))
        def _():
            pack_dq(h, 0)

        @pl.when((t == 4) | (t == 6) | (t == 10))
        def _():
            send_core(h)

        @pl.when((t == 5) | (t == 7) | (t == 9))
        def _():
            pack_dq(h, 1)
            send_far(h)

        @pl.when((t == 5) | (t == 7))
        def _():
            send_x(h)

        @pl.when((t == 8) | (t == 10))
        def _():
            send_near((t - 8) // 2)
            finish_kv((t - 8) // 2)

        @pl.when(t == 10)
        def _():
            finish_q(0)

    last = HL - 1
    last_kv[...] = all_cores(last).astype(BF16)
    start(last_x)
    r_lkv[y, 0] = last_kv[:SUB]
    pack_dq(last, 0)
    add_near(last)
    for r in range(NY):
        rows = slice(r * HS, (r + 1) * HS)
        last_q[0, r] = dq32[last, 0, rows].astype(BF16)
        for slot in range(1, 5):
            last_q[slot, r] = dq16[last, slot, rows]
    start(last_z)
    r_lq[y, 0] = last_q[0, 0]
    finish_q(1)
    start([fq_copy(r) for r in order])
    r_fq[y] = fin_q[0]
    arrive(last_x)
    for n in range(NY):
        total = r_lkv[n, 0].astype(F32)
        for slot in range(1, NX):
            total = total + r_lkv[n, slot].astype(F32)
        out_kv[last, n] = total.astype(BF16)
    arrive(last_z)
    for n in range(NY):
        total = r_lq[n, 0].astype(F32)
        for slot in range(1, 5):
            total = total + r_lq[n, slot].astype(F32)
        out_q[n, :, last * D : HL * D] = unpack(total)
    arrive([fkv_copy(h, r) for h in range(last) for r in order] + [fq_copy(r) for r in order])
    for h in range(last):
        out_kv[h] = r_kv[h]
    out_q[:, :, : last * D] = r_fq[...]

    done = [y_copy(r, kind) for r in order for kind in range(3)] + [lse_core(), lse_y()]
    for step in range(1, NZ // 2 + 1):
        for sign in (1, -1):
            done += [z_copy(step, sign, r) for r in parts(step, sign)]
            if step < NZ // 2 or sign > 0:
                done.append(s_copy(step, sign))
    done += [copy for r in range(NY) for copy in x_copies(r)]
    done += [c_copy(i) for i in range(NC)] + [kc_copy(h) for h in range(HL)]
    done += [kx_copy(h, d) for h in range(last) for d in X_SLOT if d]
    done += [q_copy(h, d) for h in range(last) for d in (2, -2, 1, -1)] + last_x + last_z
    done += [v_copy(h, i) for h in range(HL) for i in range(4)]
    done += [fkv_copy(h, r) for h in range(last) for r in order] + [fq_copy(r) for r in order]
    for copy in done:
        copy.wait_send()


def place(kv_ref, q_ref, dq_ref, dk_ref, dv_ref):
    for n in range(NY):
        for h in range(HL):
            cols = slice((n * HL + h) * D, (n * HL + h + 1) * D)
            pair = kv_ref[h, n]
            dk_ref[:, cols] = pair[:, :D]
            dv_ref[:, cols] = pair[:, D:]
        dq_ref[:, n * HL * D : (n + 1) * HL * D] = q_ref[n]


def local(queries, keys, values, attended, grad_out, logsumexp):
    dma = pltpu.SemaphoreType.DMA
    vm = pltpu.VMEM
    whole = pl.BlockSpec(memory_space=pltpu.VMEM)
    sums = pl.pallas_call(
        kernel,
        out_shape=(
            pltpu.VMEM((HL, NY, SUB, 2 * D), BF16),
            pltpu.VMEM((NY, SUB, HL * D), BF16),
        ),
        in_specs=[whole] * 6,
        out_specs=[whole] * 2,
        scratch_shapes=[
            vm((NY, HL, SUB, 2 * D), BF16),
            vm((NY, HL, SUB, 2 * D), BF16),
            vm((NY, 8, SUB), F32),
            vm((2, 2, 8, SUB), F32),
            vm((HL, NI, 2 * D), BF16),
            vm((HL, NJ, 2 * D), BF16),
            vm((2, 2, 8, SUB), F32),
            vm((2, 2, 8, SUB), F32),
            vm((NY, 8, SUB), F32),
            vm((NZ, 8, CH), F32),
            vm((8, NI), F32),
            vm((HL, D, NI), F32),
            vm((HL, NJ, 2 * D), F32),
            vm((HL, HALF, 2 * D), BF16),
            vm((HL, HALF, 2 * D), BF16),
            vm((HL, HALF - CH, 2 * D), BF16),
            vm((HL, NX - 1, CH, 2 * D), BF16),
            vm((HL, NZ, PK, 2 * D), F32),
            vm((HL, NZ, PK, 2 * D), BF16),
            vm((HL, 4, PK, 2 * D), BF16),
            vm((HL, 5, PK, 2 * D), BF16),
            vm((HL, CH, 2 * D), BF16),
            vm((NY, SUB, 2 * D), BF16),
            vm((HL - 1, NY, SUB, 2 * D), BF16),
            vm((NY, SUB, 2 * D), BF16),
            vm((HALF, 2 * D), BF16),
            vm((NY, NX, SUB, 2 * D), BF16),
            vm((5, NY, HS, 2 * D), BF16),
            vm((NY, 5, HS, 2 * D), BF16),
            dma((NY, 3)), dma((NY, 3)),
            dma((2,)), dma((2,)),
            dma((2, NZ // 2 + 1, NY)), dma((2, NZ // 2 + 1, NY)),
            dma((2, NZ // 2 + 1)), dma((2, NZ // 2 + 1)),
            dma((NX, NY)), dma((NX, NY)),
            dma((NC,)), dma((NC,)),
            dma((HL,)), dma((HL,)),
            dma((HL, NX)), dma((HL, NX)),
            dma((HL, 4)), dma((HL, 4)),
            dma((HL, 5)), dma((HL, 5)),
            dma((HL, NY)), dma((HL, NY)),
            dma((NX, NY)), dma((NX, NY)),
            dma((5, NY)), dma((5, NY)),
        ],
        compiler_params=pltpu.CompilerParams(
            collective_id=0, has_side_effects=True, vmem_limit_bytes=56 << 20
        ),
        name="attention_grad",
    )(queries, keys, values, attended, grad_out, jnp.transpose(logsumexp))
    out = jax.ShapeDtypeStruct(queries.shape, BF16)
    return pl.pallas_call(
        place, out_shape=(out, out, out), in_specs=[whole] * 2, out_specs=[whole] * 3, name="place"
    )(*[pltpu.with_memory_space_constraint(part, pltpu.VMEM) for part in sums])


def solution(mesh):
    rows = P(("ctx", "head"), None)
    return jax.shard_map(
        local,
        mesh=mesh,
        in_specs=(rows,) * 5 + (P("ctx", "head"),),
        out_specs=(rows,) * 3,
        check_vma=False,
    )
```

```python
import functools

import jax
import jax.numpy as jnp
from jax import lax
from jax.experimental import pallas as pl
from jax.experimental.pallas import tpu as pltpu
from jax.sharding import PartitionSpec as P

F32 = jnp.float32
BF16 = jnp.bfloat16
MESH = pl.DeviceIdType.MESH

NX, NY, NZ = 4, 4, 8
HL = 3
D = 64
SUB = 48
CH = NY * SUB
NI = NZ * CH
NJ = 2 * NX * CH
HALF = NJ // 2
Z_SLOT = {0: 0, 1: 1, -1: 2, 2: 3, -2: 4, 3: 5, -3: 6, 4: 7}
X_SLOT = {0: 0, 1: 1, -1: 2, 2: 3}
NC = NY + 2 * (NX - 1)
HS = SUB // 2
PK = CH // 2


def nt(a, b):
    return lax.dot_general(a, b, (((1,), (1,)), ((), ())), preferred_element_type=F32)


def tn(a, b):
    return lax.dot_general(a, b, (((0,), (0,)), ((), ())), preferred_element_type=F32)


def nn(a, b):
    return jnp.dot(a, b, preferred_element_type=F32)


def kernel(
    q_ref, k_ref, v_ref, o_ref, g_ref, lse_ref, out_kv, out_q,
    st_qg, st_kv, st_d, st_lse, qg, kv, pair, r_lse, r_d, stat, stat_all, dqt, dkv, dkv16, r_core, x16,
    r_x, dq32, dq16, r_v, r_q, fin_kv, fin_q, r_kv, r_fq, last_kv, r_lkv, last_q, r_lq,
    a_send, a_recv, l_send, l_recv, z_send, z_recv, s_send, s_recv, x_send, x_recv, c_send, c_recv,
    kc_send, kc_recv, kx_send, kx_recv, v_send, v_recv, q_send, q_recv, f_send, f_recv,
    lx_send, lx_recv, lq_send, lq_recv,
):
    c = lax.axis_index("ctx")
    g = lax.axis_index("head")
    z = c % NZ
    x = (c // NZ) % NX
    y_lo = c // (NZ * NX)
    y_hi = g // 2
    core = g % 2
    y = 2 * y_hi + y_lo

    def dev(dx=0, dy=0, dz=0, other=False):
        yy = (y + dy) % NY
        cc = (yy % 2) * (NX * NZ) + ((x + dx + NX) % NX) * NZ + (z + dz + NZ) % NZ
        return (cc, (yy // 2) * 2 + (1 - core if other else core))

    def remote(src, dst, send, recv, to):
        return pltpu.make_async_remote_copy(
            src_ref=src, dst_ref=dst, send_sem=send, recv_sem=recv, device_id=to,
            device_id_type=MESH,
        )

    def start(copies):
        for copy in copies:
            copy.start()

    def arrive(copies):
        for copy in copies:
            copy.wait_recv()

    def leave(copies):
        for copy in copies:
            copy.wait_send()

    barrier = pltpu.get_barrier_semaphore()
    peers = [dev(dy=dy) for dy in range(1, NY)] + [dev(other=True), dev(dz=1), dev(dz=-1)]
    peers += [dev(dx=d) for d in X_SLOT if d]
    for peer in peers:
        pl.semaphore_signal(barrier, inc=1, device_id=peer, device_id_type=MESH)

    def y_copy(r, kind):
        group = (y + r) % NY
        rows = pl.ds((NY - r) * SUB, SUB)
        src = (st_qg, st_kv, st_d)[kind].at[group]
        dst = (qg.at[:, rows], kv.at[:, rows], r_d.at[NY - r])[kind]
        return remote(src, dst, a_send.at[r, kind], a_recv.at[r, kind], dev(dy=r))

    def z_copy(step, sign, r):
        d = -sign * (step - 1)
        a = Z_SLOT[d]
        b = Z_SLOT[4 if step == NZ // 2 else d - sign]
        way = 0 if sign > 0 else 1
        return remote(
            qg.at[:, pl.ds(a * CH + r * SUB, SUB)], qg.at[:, pl.ds(b * CH + r * SUB, SUB)],
            z_send.at[way, step, r], z_recv.at[way, step, r], dev(dz=sign),
        )

    def x_copy(d, r):
        back = X_SLOT[2 if d == 2 else -d]
        return remote(
            kv.at[:, pl.ds(r * SUB, SUB)], kv.at[:, pl.ds(back * CH + r * SUB, SUB)],
            x_send.at[X_SLOT[d], r], x_recv.at[X_SLOT[d], r], dev(dx=d),
        )

    def x_copies(r):
        return [x_copy(d, r) for d in (2, 1, -1)]

    def parts(step, sign):
        return range(NY) if step < NZ // 2 else ((0, 1) if sign > 0 else (2, 3))

    def s_copy(step, sign):
        d = -sign * (step - 1)
        way = 0 if sign > 0 else 1
        return remote(
            stat.at[Z_SLOT[d]], stat.at[Z_SLOT[4 if step == NZ // 2 else d - sign]],
            s_send.at[way, step], s_recv.at[way, step], dev(dz=sign),
        )

    def c_copy(i):
        if i < NY:
            begin, rows = i * SUB, SUB
        else:
            begin, rows = CH + ((i - NY) // 2) * CH + (i % 2) * (CH // 2), CH // 2
        return remote(
            kv.at[:, pl.ds(begin, rows)], kv.at[:, pl.ds(HALF + begin, rows)],
            c_send.at[i], c_recv.at[i], dev(other=True),
        )

    def lse_core():
        return remote(
            st_lse.at[1 - core], pair.at[core], l_send.at[0], l_recv.at[0], dev(other=True)
        )

    def lse_y():
        there = (1 - y_lo) * (NX * NZ) + x * NZ + z
        return remote(pair.at[1 - y_lo], r_lse.at[y_lo], l_send.at[1], l_recv.at[1], (there, g))

    def stage(st, left, right):
        for n in range(NY * HL):
            cols = slice(n * D, (n + 1) * D)
            st[n // HL, n % HL] = jnp.concatenate([left[:, cols], right[:, cols]], axis=1)

    order = (1, 3, 2)
    stage(st_kv, k_ref[...], v_ref[...])
    pl.semaphore_wait(barrier, len(peers))
    start([y_copy(r, 1) for r in order])
    st_lse[...] = jnp.zeros_like(st_lse)
    for s in range(NY):
        st_lse[s % 2, s // 2, 0:HL] = lse_ref[:, s * SUB : (s + 1) * SUB]
    lse_core().start()
    pair[core] = st_lse[core]
    kv[:, 0:SUB] = st_kv[y]
    start(x_copies(0) + [c_copy(0)])
    gs = g_ref[...]
    stage(st_qg, q_ref[...] * jnp.asarray(0.125, BF16), gs)
    start([y_copy(r, 0) for r in order])
    qg[:, 0:SUB] = st_qg[y]
    start([z_copy(1, 1, 0), z_copy(1, -1, 0)])
    prod = gs.astype(F32) * o_ref[...].astype(F32)
    hi = prod.astype(BF16)
    lo = (prod - hi.astype(F32)).astype(BF16)
    row = lax.broadcasted_iota(jnp.int32, (8 * NY, NY * HL * D), 0)
    col = lax.broadcasted_iota(jnp.int32, (8 * NY, NY * HL * D), 1)
    begin = ((row // 8) * HL + row % 8) * D
    pick = ((row % 8 < HL) & (col >= begin) & (col < begin + D)).astype(F32).astype(BF16)
    deltas = nt(pick, hi) + nt(pick, lo)
    for n in range(NY):
        st_d[n] = deltas[8 * n : 8 * n + 8]
    start([y_copy(r, 2) for r in order])
    r_d[0] = st_d[y]
    dqt[...] = jnp.zeros_like(dqt)
    dkv[...] = jnp.zeros_like(dkv)
    lse_core().wait_recv()
    lse_y().start()
    r_lse[y_lo] = pair[y_lo]

    for r, kind in ((1, 1), (3, 1), (1, 0), (3, 0), (2, 1), (2, 0)):
        y_copy(NY - r, kind).wait_recv()
        if kind == 1:
            start(x_copies(r) + [c_copy(r)])
        else:
            start([z_copy(1, 1, r), z_copy(1, -1, r)])
    for r in range(1, NY):
        y_copy(r, 2).wait_recv()
    lse_y().wait_recv()
    for r in range(NY):
        from_at = (y + r) % NY
        both = jnp.concatenate([r_lse[from_at % 2, from_at // 2][:HL], r_d[r][: 8 - HL]], axis=0)
        stat[0, :, r * SUB : (r + 1) * SUB] = both
    start([s_copy(1, 1), s_copy(1, -1)])
    for i, r in enumerate((0, 1, 3, 2)):
        arrive(x_copies(r))
        if i % 2:
            start([c_copy(NY + 2 * n + i // 2) for n in range(NX - 1)])
        for sign in (1, -1):
            z_copy(1, sign, r).wait_recv()
            z_copy(2, sign, r).start()
    for sign in (1, -1):
        s_copy(1, sign).wait_recv()
        s_copy(2, sign).start()
    for r in (0, 1, 3, 2):
        for sign in (1, -1):
            z_copy(2, sign, r).wait_recv()
            z_copy(3, sign, r).start()
    for sign in (1, -1):
        s_copy(2, sign).wait_recv()
        s_copy(3, sign).start()

    def join(slots):
        for slot in slots:
            stat_all[:, slot * CH : (slot + 1) * CH] = stat[slot]

    join(range(4))

    def v_copy(h, i):
        slot = (5, 6, 7, 7)[i]
        rows = pl.ds((0, 0, 0, PK // 2)[i], (PK, PK, PK // 2, PK // 2)[i])
        return remote(
            dq16.at[h, slot, rows], r_v.at[h, i, rows], v_send.at[h, i], v_recv.at[h, i],
            dev(dz=(2, -2, 2, -2)[i]),
        )

    def q_copy(h, d):
        slot = Z_SLOT[d]
        back = Z_SLOT[-d]
        return remote(
            dq16.at[h, slot], r_q.at[h, back], q_send.at[h, slot], q_recv.at[h, slot], dev(dz=d)
        )

    def pack_dq(h, half):
        cols = slice(half * 4 * CH, (half + 1) * 4 * CH)
        block = jnp.transpose(dqt[h, :, cols]) * 0.125
        for t in range(4):
            for r in range(NY):
                at = t * CH + r * SUB
                dq32[h, 4 * half + t, r * HS : (r + 1) * HS] = jnp.concatenate(
                    [block[at : at + HS], block[at + HS : at + SUB]], axis=1
                )

    def send_far(h):
        for slot in (5, 6, 7):
            dq16[h, slot] = dq32[h, slot].astype(BF16)
        start([v_copy(h, i) for i in range(4)])

    def add_near(h):
        arrive([v_copy(h, i) for i in range(4)])
        half = PK // 2
        dq16[h, 1] = (dq32[h, 1] + r_v[h, 0].astype(F32)).astype(BF16)
        dq16[h, 2] = (dq32[h, 2] + r_v[h, 1].astype(F32)).astype(BF16)
        dq16[h, 3, :half] = (dq32[h, 3, :half] + r_v[h, 2, :half].astype(F32)).astype(BF16)
        dq16[h, 3, half:] = dq32[h, 3, half:].astype(BF16)
        dq16[h, 4, :half] = dq32[h, 4, :half].astype(BF16)
        dq16[h, 4, half:] = (dq32[h, 4, half:] + r_v[h, 3, half:].astype(F32)).astype(BF16)

    def send_near(h):
        add_near(h)
        start([q_copy(h, d) for d in (2, -2, 1, -1)])

    NEAR = (2, -2, 1, -1, 0)
    FAR_X = (2, 1, -1, 0)

    def lq_copy(d, r):
        slot = Z_SLOT[d]
        return remote(
            last_q.at[slot, r], r_lq.at[y, Z_SLOT[-d]], lq_send.at[slot, r], lq_recv.at[slot, r],
            dev(dz=d, dy=r),
        )

    def lx_copy(d, r):
        slot = X_SLOT[d]
        back = X_SLOT[2 if d == 2 else -d]
        return remote(
            last_kv.at[pl.ds(slot * CH + r * SUB, SUB)], r_lkv.at[y, back], lx_send.at[slot, r],
            lx_recv.at[slot, r], dev(dx=d, dy=r),
        )

    last_x = [lx_copy(d, r) for r in (2, 1, 3, 0) for d in FAR_X if d or r]
    last_z = [lq_copy(d, r) for r in (2, 1, 3, 0) for d in NEAR if d or r]

    def kc_copy(h):
        return remote(dkv16.at[h], r_core.at[h], kc_send.at[h], kc_recv.at[h], dev(other=True))

    def send_core(h):
        dkv16[h] = dkv[h, HALF:].astype(BF16)
        kc_copy(h).start()

    def kx_copy(h, d):
        slot = X_SLOT[d]
        back = X_SLOT[2 if d == 2 else -d]
        return remote(
            x16.at[h, pl.ds((slot - 1) * CH, CH)], r_x.at[h, back - 1], kx_send.at[h, slot],
            kx_recv.at[h, slot], dev(dx=d),
        )

    def all_cores(h):
        kc_copy(h).wait_recv()
        return dkv[h, :HALF] + r_core[h].astype(F32)

    def send_x(h):
        total = all_cores(h)
        x16[h] = total[CH:].astype(BF16)
        start([kx_copy(h, d) for d in X_SLOT if d])
        dkv[h, :CH] = total[:CH]

    def fkv_copy(h, r):
        return remote(
            fin_kv.at[h, pl.ds(r * SUB, SUB)], r_kv.at[h, y], f_send.at[h, r], f_recv.at[h, r],
            dev(dy=r),
        )

    def fq_copy(r):
        return remote(fin_q.at[r], r_fq.at[y], f_send.at[HL - 1, r], f_recv.at[HL - 1, r], dev(dy=r))

    def finish_kv(h):
        arrive([kx_copy(h, d) for d in X_SLOT if d])
        total = dkv[h, :CH]
        for slot in range(NX - 1):
            total = total + r_x[h, slot].astype(F32)
        total = total.astype(BF16)
        fin_kv[h] = total
        start([fkv_copy(h, r) for r in order])
        r_kv[h, y] = total[:SUB]

    def unpack(rows):
        return jnp.concatenate([rows[:, :D], rows[:, D:]], axis=0).astype(BF16)

    def finish_q(h):
        arrive([q_copy(h, d) for d in (2, -2, 1, -1)])
        total = dq32[h, 0]
        for slot in range(1, 5):
            total = total + r_q[h, slot].astype(F32)
        for r in range(NY):
            fin_q[r, :, h * D : (h + 1) * D] = unpack(total[r * HS : (r + 1) * HS])

    lane = lax.broadcasted_iota(jnp.int32, (HALF, 2 * D), 1)

    @pl.loop(0, 4 * HL)
    def _(t):
        h = jnp.where(t < 4, t % 2, (t - 4) // 2)
        h = jnp.where(t < 8, h, 2)
        late = jnp.where((t >= 4) & (t < 10), 1, 0)
        sib = jnp.where((t == 3) | ((t >= 2) & (t % 2 == 0)), 1, 0)

        @pl.when(t == 2)
        def _():
            arrive([c_copy(i) for i in range(NC)])
            for r in range(NY):
                for sign in (1, -1):
                    z_copy(3, sign, r).wait_recv()
                    if r in parts(4, sign):
                        z_copy(4, sign, r).start()
            arrive([s_copy(3, 1), s_copy(3, -1)])
            s_copy(4, 1).start()

        @pl.when(t == 4)
        def _():
            arrive([z_copy(4, sign, r) for sign in (1, -1) for r in parts(4, sign)])
            s_copy(4, 1).wait_recv()
            join(range(4, 8))

        cols = pl.ds(pl.multiple_of(late * (4 * CH), 4 * CH), 4 * CH)
        js = pl.ds(pl.multiple_of(sib * HALF, HALF), HALF)
        norms = stat_all[pl.ds(h, 1), cols]
        dels = stat_all[pl.ds(HL + h, 1), cols]
        rows_q = qg[h, cols]
        both = kv[h, js]
        zero = jnp.zeros_like(both)
        scores = nt(jnp.where(lane < D, both, zero), rows_q)
        dweights = nt(jnp.where(lane < D, zero, both), rows_q)
        weights = jnp.exp(scores - norms)
        dscores = (weights * (dweights - dels)).astype(BF16)
        low = weights.astype(BF16)
        dkv[h, js] += jnp.where(lane < D, nn(dscores, rows_q), nn(low, rows_q))
        dqt[h, :, cols] += tn(both, dscores)[:D]

        @pl.when((t == 2) | (t == 3))
        def _():
            pack_dq(h, 0)

        @pl.when((t == 4) | (t == 6) | (t == 10))
        def _():
            send_core(h)

        @pl.when((t == 5) | (t == 7) | (t == 9))
        def _():
            pack_dq(h, 1)
            send_far(h)

        @pl.when((t == 5) | (t == 7))
        def _():
            send_x(h)

        @pl.when((t == 8) | (t == 9))
        def _():
            send_near(t - 8)
            finish_kv(t - 8)

        @pl.when(t == 10)
        def _():
            finish_q(0)

    last = HL - 1
    pack_dq(last, 0)
    last_kv[...] = all_cores(last).astype(BF16)
    start(last_x)
    r_lkv[y, 0] = last_kv[:SUB]
    finish_q(1)
    start([fq_copy(r) for r in order])
    r_fq[y] = fin_q[0]
    add_near(last)
    for r in range(NY):
        rows = slice(r * HS, (r + 1) * HS)
        last_q[0, r] = dq32[last, 0, rows].astype(BF16)
        for slot in range(1, 5):
            last_q[slot, r] = dq16[last, slot, rows]
    start(last_z)
    r_lq[y, 0] = last_q[0, 0]
    done = [y_copy(r, kind) for r in order for kind in range(3)] + [lse_core(), lse_y()]
    for step in range(1, NZ // 2 + 1):
        for sign in (1, -1):
            done += [z_copy(step, sign, r) for r in parts(step, sign)]
            if step < NZ // 2 or sign > 0:
                done.append(s_copy(step, sign))
    done += [copy for r in range(NY) for copy in x_copies(r)]
    done += [c_copy(i) for i in range(NC)] + [kc_copy(h) for h in range(HL)]
    done += [kx_copy(h, d) for h in range(last) for d in X_SLOT if d]
    done += [q_copy(h, d) for h in range(last) for d in (2, -2, 1, -1)]
    done += [v_copy(h, i) for h in range(HL) for i in range(4)]
    leave(done)
    leave(last_x)
    arrive(last_x)
    for n in range(NY):
        total = r_lkv[n, 0].astype(F32)
        for slot in range(1, NX):
            total = total + r_lkv[n, slot].astype(F32)
        out_kv[last, n] = total.astype(BF16)
    leave(last_z)
    arrive(last_z)
    for n in range(NY):
        total = r_lq[n, 0].astype(F32)
        for slot in range(1, 5):
            total = total + r_lq[n, slot].astype(F32)
        out_q[n, :, last * D : HL * D] = unpack(total)
    fc = [fkv_copy(h, r) for h in range(last) for r in order] + [fq_copy(r) for r in order]
    arrive(fc)
    for h in range(last):
        out_kv[h] = r_kv[h]
    out_q[:, :, : last * D] = r_fq[...]
    leave(fc)


def place(kv_ref, q_ref, dq_ref, dk_ref, dv_ref):
    for n in range(NY):
        for h in range(HL):
            cols = slice((n * HL + h) * D, (n * HL + h + 1) * D)
            pair = kv_ref[h, n]
            dk_ref[:, cols] = pair[:, :D]
            dv_ref[:, cols] = pair[:, D:]
        dq_ref[:, n * HL * D : (n + 1) * HL * D] = q_ref[n]


def local(queries, keys, values, attended, grad_out, logsumexp):
    dma = pltpu.SemaphoreType.DMA
    vm = pltpu.VMEM
    whole = pl.BlockSpec(memory_space=pltpu.VMEM)
    sums = pl.pallas_call(
        kernel,
        out_shape=(
            pltpu.VMEM((HL, NY, SUB, 2 * D), BF16),
            pltpu.VMEM((NY, SUB, HL * D), BF16),
        ),
        in_specs=[whole] * 6,
        out_specs=[whole] * 2,
        scratch_shapes=[
            vm((NY, HL, SUB, 2 * D), BF16),
            vm((NY, HL, SUB, 2 * D), BF16),
            vm((NY, 8, SUB), F32),
            vm((2, 2, 8, SUB), F32),
            vm((HL, NI, 2 * D), BF16),
            vm((HL, NJ, 2 * D), BF16),
            vm((2, 2, 8, SUB), F32),
            vm((2, 2, 8, SUB), F32),
            vm((NY, 8, SUB), F32),
            vm((NZ, 8, CH), F32),
            vm((8, NI), F32),
            vm((HL, D, NI), F32),
            vm((HL, NJ, 2 * D), F32),
            vm((HL, HALF, 2 * D), BF16),
            vm((HL, HALF, 2 * D), BF16),
            vm((HL, HALF - CH, 2 * D), BF16),
            vm((HL, NX - 1, CH, 2 * D), BF16),
            vm((HL, NZ, PK, 2 * D), F32),
            vm((HL, NZ, PK, 2 * D), BF16),
            vm((HL, 4, PK, 2 * D), BF16),
            vm((HL, 5, PK, 2 * D), BF16),
            vm((HL, CH, 2 * D), BF16),
            vm((NY, SUB, 2 * D), BF16),
            vm((HL - 1, NY, SUB, 2 * D), BF16),
            vm((NY, SUB, 2 * D), BF16),
            vm((HALF, 2 * D), BF16),
            vm((NY, NX, SUB, 2 * D), BF16),
            vm((5, NY, HS, 2 * D), BF16),
            vm((NY, 5, HS, 2 * D), BF16),
            dma((NY, 3)), dma((NY, 3)),
            dma((2,)), dma((2,)),
            dma((2, NZ // 2 + 1, NY)), dma((2, NZ // 2 + 1, NY)),
            dma((2, NZ // 2 + 1)), dma((2, NZ // 2 + 1)),
            dma((NX, NY)), dma((NX, NY)),
            dma((NC,)), dma((NC,)),
            dma((HL,)), dma((HL,)),
            dma((HL, NX)), dma((HL, NX)),
            dma((HL, 4)), dma((HL, 4)),
            dma((HL, 5)), dma((HL, 5)),
            dma((HL, NY)), dma((HL, NY)),
            dma((NX, NY)), dma((NX, NY)),
            dma((5, NY)), dma((5, NY)),
        ],
        compiler_params=pltpu.CompilerParams(
            collective_id=0, has_side_effects=True, vmem_limit_bytes=56 << 20
        ),
        name="attention_grad",
    )(queries, keys, values, attended, grad_out, jnp.transpose(logsumexp))
    out = jax.ShapeDtypeStruct(queries.shape, BF16)
    return pl.pallas_call(
        place, out_shape=(out, out, out), in_specs=[whole] * 2, out_specs=[whole] * 3, name="place"
    )(*[pltpu.with_memory_space_constraint(part, pltpu.VMEM) for part in sums])


def solution(mesh):
    rows = P(("ctx", "head"), None)
    return jax.shard_map(
        local,
        mesh=mesh,
        in_specs=(rows,) * 5 + (P("ctx", "head"),),
        out_specs=(rows,) * 3,
        check_vma=False,
    )
```

```python
import functools

import jax
import jax.numpy as jnp
from jax import lax
from jax.experimental import pallas as pl
from jax.experimental.pallas import tpu as pltpu
from jax.sharding import PartitionSpec as P

F32 = jnp.float32
BF16 = jnp.bfloat16
MESH = pl.DeviceIdType.MESH

NX, NY, NZ = 4, 4, 8
HL = 3
D = 64
SUB = 48
CH = NY * SUB
NI = NZ * CH
NJ = 2 * NX * CH
HALF = NJ // 2
Z_SLOT = {0: 0, 1: 1, -1: 2, 2: 3, -2: 4, 3: 5, -3: 6, 4: 7}
X_SLOT = {0: 0, 1: 1, -1: 2, 2: 3}
NC = NY + 2 * (NX - 1)
HS = SUB // 2
PK = CH // 2


def nt(a, b):
    return lax.dot_general(a, b, (((1,), (1,)), ((), ())), preferred_element_type=F32)


def tn(a, b):
    return lax.dot_general(a, b, (((0,), (0,)), ((), ())), preferred_element_type=F32)


def nn(a, b):
    return jnp.dot(a, b, preferred_element_type=F32)


def kernel(
    q_ref, k_ref, v_ref, o_ref, g_ref, lse_ref, out_kv, out_q,
    st_qg, st_kv, st_d, st_lse, qg, kv, pair, r_lse, r_d, stat, stat_all, dqt, dkv, dkv16, r_core, x16,
    r_x, dq32, dq16, r_v, r_q, fin_kv, fin_q, r_kv, r_fq, last_kv, r_lkv, last_q, r_lq,
    a_send, a_recv, l_send, l_recv, z_send, z_recv, s_send, s_recv, x_send, x_recv, c_send, c_recv,
    kc_send, kc_recv, kx_send, kx_recv, v_send, v_recv, q_send, q_recv, f_send, f_recv,
    lx_send, lx_recv, lq_send, lq_recv,
):
    c = lax.axis_index("ctx")
    g = lax.axis_index("head")
    z = c % NZ
    x = (c // NZ) % NX
    y_lo = c // (NZ * NX)
    y_hi = g // 2
    core = g % 2
    y = 2 * y_hi + y_lo

    def dev(dx=0, dy=0, dz=0, other=False):
        yy = (y + dy) % NY
        cc = (yy % 2) * (NX * NZ) + ((x + dx + NX) % NX) * NZ + (z + dz + NZ) % NZ
        return (cc, (yy // 2) * 2 + (1 - core if other else core))

    def remote(src, dst, send, recv, to):
        return pltpu.make_async_remote_copy(
            src_ref=src, dst_ref=dst, send_sem=send, recv_sem=recv, device_id=to,
            device_id_type=MESH,
        )

    def start(copies):
        for copy in copies:
            copy.start()

    def arrive(copies):
        for copy in copies:
            copy.wait_recv()

    def leave(copies):
        for copy in copies:
            copy.wait_send()

    barrier = pltpu.get_barrier_semaphore()
    peers = [dev(dy=dy) for dy in range(1, NY)] + [dev(other=True), dev(dz=1), dev(dz=-1)]
    peers += [dev(dx=d) for d in X_SLOT if d]
    for peer in peers:
        pl.semaphore_signal(barrier, inc=1, device_id=peer, device_id_type=MESH)

    def y_copy(r, kind):
        group = (y + r) % NY
        rows = pl.ds((NY - r) * SUB, SUB)
        src = (st_qg, st_kv, st_d)[kind].at[group]
        dst = (qg.at[:, rows], kv.at[:, rows], r_d.at[NY - r])[kind]
        return remote(src, dst, a_send.at[r, kind], a_recv.at[r, kind], dev(dy=r))

    def z_copy(step, sign, r):
        d = -sign * (step - 1)
        a = Z_SLOT[d]
        b = Z_SLOT[4 if step == NZ // 2 else d - sign]
        way = 0 if sign > 0 else 1
        return remote(
            qg.at[:, pl.ds(a * CH + r * SUB, SUB)], qg.at[:, pl.ds(b * CH + r * SUB, SUB)],
            z_send.at[way, step, r], z_recv.at[way, step, r], dev(dz=sign),
        )

    def x_copy(d, r):
        back = X_SLOT[2 if d == 2 else -d]
        return remote(
            kv.at[:, pl.ds(r * SUB, SUB)], kv.at[:, pl.ds(back * CH + r * SUB, SUB)],
            x_send.at[X_SLOT[d], r], x_recv.at[X_SLOT[d], r], dev(dx=d),
        )

    def x_copies(r):
        return [x_copy(d, r) for d in (2, 1, -1)]

    def parts(step, sign):
        return range(NY) if step < NZ // 2 else ((0, 1) if sign > 0 else (2, 3))

    def s_copy(step, sign):
        d = -sign * (step - 1)
        way = 0 if sign > 0 else 1
        return remote(
            stat.at[Z_SLOT[d]], stat.at[Z_SLOT[4 if step == NZ // 2 else d - sign]],
            s_send.at[way, step], s_recv.at[way, step], dev(dz=sign),
        )

    def c_copy(i):
        if i < NY:
            begin, rows = i * SUB, SUB
        else:
            begin, rows = CH + ((i - NY) // 2) * CH + (i % 2) * (CH // 2), CH // 2
        return remote(
            kv.at[:, pl.ds(begin, rows)], kv.at[:, pl.ds(HALF + begin, rows)],
            c_send.at[i], c_recv.at[i], dev(other=True),
        )

    def lse_core():
        return remote(
            st_lse.at[1 - core], pair.at[core], l_send.at[0], l_recv.at[0], dev(other=True)
        )

    def lse_y():
        there = (1 - y_lo) * (NX * NZ) + x * NZ + z
        return remote(pair.at[1 - y_lo], r_lse.at[y_lo], l_send.at[1], l_recv.at[1], (there, g))

    def stage(st, left, right):
        for n in range(NY * HL):
            cols = slice(n * D, (n + 1) * D)
            st[n // HL, n % HL] = jnp.concatenate([left[:, cols], right[:, cols]], axis=1)

    order = (1, 3, 2)
    stage(st_kv, k_ref[...], v_ref[...])
    pl.semaphore_wait(barrier, len(peers))
    start([y_copy(r, 1) for r in order])
    st_lse[...] = jnp.zeros_like(st_lse)
    for s in range(NY):
        st_lse[s % 2, s // 2, 0:HL] = lse_ref[:, s * SUB : (s + 1) * SUB]
    lse_core().start()
    pair[core] = st_lse[core]
    kv[:, 0:SUB] = st_kv[y]
    start(x_copies(0) + [c_copy(0)])
    gs = g_ref[...]
    stage(st_qg, q_ref[...] * jnp.asarray(0.125, BF16), gs)
    start([y_copy(r, 0) for r in order])
    qg[:, 0:SUB] = st_qg[y]
    start([z_copy(1, 1, 0), z_copy(1, -1, 0)])
    prod = gs.astype(F32) * o_ref[...].astype(F32)
    hi = prod.astype(BF16)
    lo = (prod - hi.astype(F32)).astype(BF16)
    row = lax.broadcasted_iota(jnp.int32, (8 * NY, NY * HL * D), 0)
    col = lax.broadcasted_iota(jnp.int32, (8 * NY, NY * HL * D), 1)
    begin = ((row // 8) * HL + row % 8) * D
    pick = ((row % 8 < HL) & (col >= begin) & (col < begin + D)).astype(F32).astype(BF16)
    deltas = nt(pick, hi) + nt(pick, lo)
    for n in range(NY):
        st_d[n] = deltas[8 * n : 8 * n + 8]
    start([y_copy(r, 2) for r in order])
    r_d[0] = st_d[y]
    dqt[...] = jnp.zeros_like(dqt)
    dkv[...] = jnp.zeros_like(dkv)
    lse_core().wait_recv()
    lse_y().start()
    r_lse[y_lo] = pair[y_lo]

    for r, kind in ((1, 1), (3, 1), (1, 0), (3, 0), (2, 1), (2, 0)):
        y_copy(NY - r, kind).wait_recv()
        if kind == 1:
            start(x_copies(r) + [c_copy(r)])
        else:
            start([z_copy(1, 1, r), z_copy(1, -1, r)])
    for r in range(1, NY):
        y_copy(r, 2).wait_recv()
    lse_y().wait_recv()
    for r in range(NY):
        from_at = (y + r) % NY
        both = jnp.concatenate([r_lse[from_at % 2, from_at // 2][:HL], r_d[r][: 8 - HL]], axis=0)
        stat[0, :, r * SUB : (r + 1) * SUB] = both
    start([s_copy(1, 1), s_copy(1, -1)])
    for i, r in enumerate((0, 1, 3, 2)):
        arrive(x_copies(r))
        if i % 2:
            start([c_copy(NY + 2 * n + i // 2) for n in range(NX - 1)])
        for sign in (1, -1):
            z_copy(1, sign, r).wait_recv()
            z_copy(2, sign, r).start()
    for sign in (1, -1):
        s_copy(1, sign).wait_recv()
        s_copy(2, sign).start()
    for r in (0, 1, 3, 2):
        for sign in (1, -1):
            z_copy(2, sign, r).wait_recv()
            z_copy(3, sign, r).start()
    for sign in (1, -1):
        s_copy(2, sign).wait_recv()
        s_copy(3, sign).start()

    def join(slots):
        for slot in slots:
            stat_all[:, slot * CH : (slot + 1) * CH] = stat[slot]

    join(range(4))

    def v_copy(h, i):
        slot = (5, 6, 7, 7)[i]
        rows = pl.ds((0, 0, 0, PK // 2)[i], (PK, PK, PK // 2, PK // 2)[i])
        return remote(
            dq16.at[h, slot, rows], r_v.at[h, i, rows], v_send.at[h, i], v_recv.at[h, i],
            dev(dz=(2, -2, 2, -2)[i]),
        )

    def q_copy(h, d):
        slot = Z_SLOT[d]
        back = Z_SLOT[-d]
        return remote(
            dq16.at[h, slot], r_q.at[h, back], q_send.at[h, slot], q_recv.at[h, slot], dev(dz=d)
        )

    def pack_dq(h, half):
        cols = slice(half * 4 * CH, (half + 1) * 4 * CH)
        block = jnp.transpose(dqt[h, :, cols]) * 0.125
        for t in range(4):
            for r in range(NY):
                at = t * CH + r * SUB
                dq32[h, 4 * half + t, r * HS : (r + 1) * HS] = jnp.concatenate(
                    [block[at : at + HS], block[at + HS : at + SUB]], axis=1
                )

    def send_far(h):
        for slot in (5, 6, 7):
            dq16[h, slot] = dq32[h, slot].astype(BF16)
        start([v_copy(h, i) for i in range(4)])

    def add_near(h):
        arrive([v_copy(h, i) for i in range(4)])
        half = PK // 2
        dq16[h, 1] = (dq32[h, 1] + r_v[h, 0].astype(F32)).astype(BF16)
        dq16[h, 2] = (dq32[h, 2] + r_v[h, 1].astype(F32)).astype(BF16)
        dq16[h, 3, :half] = (dq32[h, 3, :half] + r_v[h, 2, :half].astype(F32)).astype(BF16)
        dq16[h, 3, half:] = dq32[h, 3, half:].astype(BF16)
        dq16[h, 4, :half] = dq32[h, 4, :half].astype(BF16)
        dq16[h, 4, half:] = (dq32[h, 4, half:] + r_v[h, 3, half:].astype(F32)).astype(BF16)

    def send_near(h):
        add_near(h)
        start([q_copy(h, d) for d in (2, -2, 1, -1)])

    last = HL - 1
    NEAR = (2, -2, 1, -1, 0)
    FAR_X = (2, 1, -1, 0)

    def lq_copy(d, r):
        slot = Z_SLOT[d]
        return remote(
            last_q.at[slot, r], r_lq.at[y, Z_SLOT[-d]], lq_send.at[slot, r], lq_recv.at[slot, r],
            dev(dz=d, dy=r),
        )

    def lx_copy(d, r):
        slot = X_SLOT[d]
        back = X_SLOT[2 if d == 2 else -d]
        return remote(
            last_kv.at[pl.ds(slot * CH + r * SUB, SUB)], r_lkv.at[y, back], lx_send.at[slot, r],
            lx_recv.at[slot, r], dev(dx=d, dy=r),
        )

    last_x = [lx_copy(d, r) for r in (2, 1, 3, 0) for d in FAR_X if d or r]
    last_z = [lq_copy(d, r) for r in (2, 1, 3, 0) for d in NEAR if d or r]

    def kc_copy(h):
        return remote(dkv16.at[h], r_core.at[h], kc_send.at[h], kc_recv.at[h], dev(other=True))

    def send_core(h):
        dkv16[h] = dkv[h, HALF:].astype(BF16)
        kc_copy(h).start()

    def kx_copy(h, d):
        slot = X_SLOT[d]
        back = X_SLOT[2 if d == 2 else -d]
        return remote(
            x16.at[h, pl.ds((slot - 1) * CH, CH)], r_x.at[h, back - 1], kx_send.at[h, slot],
            kx_recv.at[h, slot], dev(dx=d),
        )

    def all_cores(h):
        kc_copy(h).wait_recv()
        return dkv[h, :HALF] + r_core[h].astype(F32)

    def send_x(h):
        total = all_cores(h)
        x16[h] = total[CH:].astype(BF16)
        start([kx_copy(h, d) for d in X_SLOT if d])
        dkv[h, :CH] = total[:CH]

    def fkv_copy(h, r):
        return remote(
            fin_kv.at[h, pl.ds(r * SUB, SUB)], r_kv.at[h, y], f_send.at[h, r], f_recv.at[h, r],
            dev(dy=r),
        )

    def fq_copy(h, r):
        return remote(
            fin_q.at[h, r], r_fq.at[h, y], f_send.at[last + h, r], f_recv.at[last + h, r],
            dev(dy=r),
        )

    def finish_kv(h):
        arrive([kx_copy(h, d) for d in X_SLOT if d])
        total = dkv[h, :CH]
        for slot in range(NX - 1):
            total = total + r_x[h, slot].astype(F32)
        total = total.astype(BF16)
        fin_kv[h] = total
        start([fkv_copy(h, r) for r in order])
        r_kv[h, y] = total[:SUB]

    def unpack(rows):
        return jnp.concatenate([rows[:, :D], rows[:, D:]], axis=0).astype(BF16)

    def finish_q(h):
        arrive([q_copy(h, d) for d in (2, -2, 1, -1)])
        total = dq32[h, 0]
        for slot in range(1, 5):
            total = total + r_q[h, slot].astype(F32)
        for r in range(NY):
            fin_q[h, r] = unpack(total[r * HS : (r + 1) * HS])
        start([fq_copy(h, r) for r in order])
        r_fq[h, y] = fin_q[h, 0]

    lane = lax.broadcasted_iota(jnp.int32, (HALF, 2 * D), 1)

    @pl.loop(0, 4 * HL)
    def _(t):
        h = jnp.where(t < 4, t % 2, (t - 4) // 2)
        h = jnp.where(t < 8, h, 2)
        late = jnp.where((t >= 4) & (t < 10), 1, 0)
        sib = jnp.where((t == 3) | ((t >= 2) & (t % 2 == 0)), 1, 0)

        @pl.when(t == 2)
        def _():
            arrive([c_copy(i) for i in range(NC)])
            for r in range(NY):
                for sign in (1, -1):
                    z_copy(3, sign, r).wait_recv()
                    if r in parts(4, sign):
                        z_copy(4, sign, r).start()
            arrive([s_copy(3, 1), s_copy(3, -1)])
            s_copy(4, 1).start()

        @pl.when(t == 4)
        def _():
            arrive([z_copy(4, sign, r) for sign in (1, -1) for r in parts(4, sign)])
            s_copy(4, 1).wait_recv()
            join(range(4, 8))

        cols = pl.ds(pl.multiple_of(late * (4 * CH), 4 * CH), 4 * CH)
        js = pl.ds(pl.multiple_of(sib * HALF, HALF), HALF)
        norms = stat_all[pl.ds(h, 1), cols]
        dels = stat_all[pl.ds(HL + h, 1), cols]
        rows_q = qg[h, cols]
        both = kv[h, js]
        zero = jnp.zeros_like(both)
        scores = nt(jnp.where(lane < D, both, zero), rows_q)
        dweights = nt(jnp.where(lane < D, zero, both), rows_q)
        weights = jnp.exp(scores - norms)
        dscores = (weights * (dweights - dels)).astype(BF16)
        low = weights.astype(BF16)
        dkv[h, js] += jnp.where(lane < D, nn(dscores, rows_q), nn(low, rows_q))
        dqt[h, :, cols] += tn(both, dscores)[:D]

        @pl.when((t == 2) | (t == 3))
        def _():
            pack_dq(h, 0)

        @pl.when((t == 4) | (t == 6) | (t == 10))
        def _():
            send_core(h)

        @pl.when((t == 5) | (t == 7) | (t == 9))
        def _():
            pack_dq(h, 1)
            send_far(h)

        @pl.when((t == 5) | (t == 7))
        def _():
            send_x(h)

        @pl.when((t == 8) | (t == 9))
        def _():
            send_near(t - 8)
            finish_kv(t - 8)

        @pl.when(t == 10)
        def _():
            finish_q(0)

    pack_dq(last, 0)
    last_kv[...] = all_cores(last).astype(BF16)
    start(last_x)
    r_lkv[y, 0] = last_kv[:SUB]
    add_near(last)
    for r in range(NY):
        rows = slice(r * HS, (r + 1) * HS)
        last_q[0, r] = dq32[last, 0, rows].astype(BF16)
        for slot in range(1, 5):
            last_q[slot, r] = dq16[last, slot, rows]
    start(last_z)
    r_lq[y, 0] = last_q[0, 0]
    done = [y_copy(r, kind) for r in order for kind in range(3)] + [lse_core(), lse_y()]
    for step in range(1, NZ // 2 + 1):
        for sign in (1, -1):
            done += [z_copy(step, sign, r) for r in parts(step, sign)]
            if step < NZ // 2 or sign > 0:
                done.append(s_copy(step, sign))
    done += [copy for r in range(NY) for copy in x_copies(r)]
    done += [c_copy(i) for i in range(NC)] + [kc_copy(h) for h in range(HL)]
    done += [kx_copy(h, d) for h in range(last) for d in X_SLOT if d]
    done += [q_copy(h, d) for h in range(last) for d in (2, -2, 1, -1)]
    done += [v_copy(h, i) for h in range(HL) for i in range(4)]
    leave(done)
    finish_q(1)
    leave(last_x)
    arrive(last_x)
    for n in range(NY):
        total = r_lkv[n, 0].astype(F32)
        for slot in range(1, NX):
            total = total + r_lkv[n, slot].astype(F32)
        out_kv[last, n] = total.astype(BF16)
    leave(last_z)
    arrive(last_z)
    for n in range(NY):
        total = r_lq[n, 0].astype(F32)
        for slot in range(1, 5):
            total = total + r_lq[n, slot].astype(F32)
        out_q[n, :, last * D : HL * D] = unpack(total)
    fc = [fkv_copy(h, r) for h in range(last) for r in order] + [fq_copy(h, r) for h in range(last) for r in order]
    arrive(fc)
    for h in range(last):
        out_kv[h] = r_kv[h]
    for h in range(last):
        out_q[:, :, h * D : (h + 1) * D] = r_fq[h]
    leave(fc)


def place(kv_ref, q_ref, dq_ref, dk_ref, dv_ref):
    for n in range(NY):
        for h in range(HL):
            cols = slice((n * HL + h) * D, (n * HL + h + 1) * D)
            pair = kv_ref[h, n]
            dk_ref[:, cols] = pair[:, :D]
            dv_ref[:, cols] = pair[:, D:]
        dq_ref[:, n * HL * D : (n + 1) * HL * D] = q_ref[n]


def local(queries, keys, values, attended, grad_out, logsumexp):
    dma = pltpu.SemaphoreType.DMA
    vm = pltpu.VMEM
    whole = pl.BlockSpec(memory_space=pltpu.VMEM)
    sums = pl.pallas_call(
        kernel,
        out_shape=(
            pltpu.VMEM((HL, NY, SUB, 2 * D), BF16),
            pltpu.VMEM((NY, SUB, HL * D), BF16),
        ),
        in_specs=[whole] * 6,
        out_specs=[whole] * 2,
        scratch_shapes=[
            vm((NY, HL, SUB, 2 * D), BF16),
            vm((NY, HL, SUB, 2 * D), BF16),
            vm((NY, 8, SUB), F32),
            vm((2, 2, 8, SUB), F32),
            vm((HL, NI, 2 * D), BF16),
            vm((HL, NJ, 2 * D), BF16),
            vm((2, 2, 8, SUB), F32),
            vm((2, 2, 8, SUB), F32),
            vm((NY, 8, SUB), F32),
            vm((NZ, 8, CH), F32),
            vm((8, NI), F32),
            vm((HL, D, NI), F32),
            vm((HL, NJ, 2 * D), F32),
            vm((HL, HALF, 2 * D), BF16),
            vm((HL, HALF, 2 * D), BF16),
            vm((HL, HALF - CH, 2 * D), BF16),
            vm((HL, NX - 1, CH, 2 * D), BF16),
            vm((HL, NZ, PK, 2 * D), F32),
            vm((HL, NZ, PK, 2 * D), BF16),
            vm((HL, 4, PK, 2 * D), BF16),
            vm((HL, 5, PK, 2 * D), BF16),
            vm((HL, CH, 2 * D), BF16),
            vm((HL - 1, NY, SUB, D), BF16),
            vm((HL - 1, NY, SUB, 2 * D), BF16),
            vm((HL - 1, NY, SUB, D), BF16),
            vm((HALF, 2 * D), BF16),
            vm((NY, NX, SUB, 2 * D), BF16),
            vm((5, NY, HS, 2 * D), BF16),
            vm((NY, 5, HS, 2 * D), BF16),
            dma((NY, 3)), dma((NY, 3)),
            dma((2,)), dma((2,)),
            dma((2, NZ // 2 + 1, NY)), dma((2, NZ // 2 + 1, NY)),
            dma((2, NZ // 2 + 1)), dma((2, NZ // 2 + 1)),
            dma((NX, NY)), dma((NX, NY)),
            dma((NC,)), dma((NC,)),
            dma((HL,)), dma((HL,)),
            dma((HL, NX)), dma((HL, NX)),
            dma((HL, 4)), dma((HL, 4)),
            dma((HL, 5)), dma((HL, 5)),
            dma((2 * HL - 2, NY)), dma((2 * HL - 2, NY)),
            dma((NX, NY)), dma((NX, NY)),
            dma((5, NY)), dma((5, NY)),
        ],
        compiler_params=pltpu.CompilerParams(
            collective_id=0, has_side_effects=True, vmem_limit_bytes=56 << 20
        ),
        name="attention_grad",
    )(queries, keys, values, attended, grad_out, jnp.transpose(logsumexp))
    out = jax.ShapeDtypeStruct(queries.shape, BF16)
    return pl.pallas_call(
        place, out_shape=(out, out, out), in_specs=[whole] * 2, out_specs=[whole] * 3, name="place"
    )(*[pltpu.with_memory_space_constraint(part, pltpu.VMEM) for part in sums])


def solution(mesh):
    rows = P(("ctx", "head"), None)
    return jax.shard_map(
        local,
        mesh=mesh,
        in_specs=(rows,) * 5 + (P("ctx", "head"),),
        out_specs=(rows,) * 3,
        check_vma=False,
    )
```
